256 devices in a mesh: tok: 32 (over x, y, core), blk: 8 (over z).
Axes of the slice: x: 4, y: 4, z: 8, core: 2. Of those that a mesh axis runs over, the one named last changes fastest.
Arguments:
- attn_out: bfloat16 [32768, 1536], P(('tok', 'blk')), may hold values from -6 to 6
- resid: bfloat16 [32768, 1536], P(('tok', 'blk')), may hold values from -6 to 6
- w_o: bfloat16 [1536, 1536], replicated, may hold values from -0.15625 to 0.15625
- norm1_gain: float32 [1536], replicated, may hold values from 0.1 to 1.9
- router_w: float32 [1536, 40], replicated, may hold values from -32 to 32
- route_slot: int32 [32768, 8], P(('tok', 'blk')), may hold values from 0 to 63, all different within a row; in each aligned block of 128 rows (0 to 127, 128 to 255, ...) at most 32 rows name the same one
- slot_expert: int32 [64], replicated, may hold values from 0 to 39, as said below
- keep: int32 [32768], P(('tok', 'blk')), may hold values 0 or 1
- w_gate: bfloat16 [64, 1536, 512], P('tok', 'blk'), may hold values from -0.15625 to 0.15625
- w_up: bfloat16 [64, 1536, 512], P('tok', 'blk'), may hold values from -0.15625 to 0.15625
- w_down: bfloat16 [64, 1536, 512], P('tok', 'blk'), may hold values from -0.25 to 0.25
- norm2_gain: float32 [1536], replicated, may hold values from 0.1 to 1.9
Outputs:
- layer_out: bfloat16 [32768, 1536], P(('tok', 'blk'))
The draws below stay inside these ranges and needn't reach their ends.
Inputs may be any that keep to these rules, and one draw needn't show every extreme that they name: `route_slot`: each row names 8 different slots; among the 128 rows of one device (aligned blocks of rows), no slot is named more than 32 times, a bound that some block reaches. `slot_expert`: every expert is named by one slot or more.
All inputs are finite; a program needn't handle non-finite values. No bound on the sum of `keep` on one device may be relied on, other than what follows from the above.
Results may differ from the reference program's by a relative error of at most 0.0099.
Values may be sent and summed in bfloat16 or wider, within the bound.
No kernel may reach another device: no remote copies, remote signals or barrier semaphores. Data moves between devices by JAX's collectives and lax.ppermute only.
A program may use at most 128 MiB of HBM per device.

```python
import math
import jax
import jax.numpy as jnp
import numpy as np
from jax import lax

D = 1536
HD = 1536
FF = 512
EXPERTS = 40
TOP = 8
ROWS_DEV = 128
SLOTS = 64
CAP = 32
TOKENS = 32768


def draw_router_w(key, part):
    values = jax.random.normal(key, (D, EXPERTS), jnp.float32) * D ** (-0.5)
    return jnp.clip(values, -32.0, 32.0)


def draw_slot_expert(key, part):
    first = jax.random.permutation(jax.random.fold_in(key, 1), EXPERTS).astype(jnp.int32)
    extra = jax.random.randint(jax.random.fold_in(key, 2), (SLOTS - EXPERTS,), 0, EXPERTS).astype(jnp.int32)
    joined = jnp.concatenate([first, extra])
    return jax.random.permutation(jax.random.fold_in(key, 5), joined).astype(jnp.int32)


def with_ends(array, key, least, high):
    longest = array.shape.index(max(array.shape))
    spots = []
    for shift in (0, 1):
        where = [jax.random.randint(jax.random.fold_in(key, axis), (), 0, length) for axis, length in enumerate(array.shape)]
        where[longest] = (where[longest] + shift) % array.shape[longest]
        spots.append(tuple(where))
    return array.at[spots[0]].set(least).at[spots[1]].set(high)


def shard_levels(own_key, shape, shards, least, high):
    factor_of, own = 1.0, jax.random.fold_in(own_key, 6)
    for axis_at, parts in shards:
        steps = jnp.exp(jax.random.uniform(jax.random.fold_in(own, axis_at), (parts,), jnp.float32, least / len(shards), high / len(shards)))
        factor_of = factor_of * jnp.repeat(steps, shape[axis_at] // parts).reshape([-1 if axis == axis_at else 1 for axis in range(len(shape))])
    return factor_of


def routed_block(rng, own, number, rows, count, top, most, skew):
    sequence = jax.random.permutation(rng, count)
    crowded, ordinary = portions_of(count, rows * top, most, skew, True), portions_of(count, rows * top, most, skew, False)
    places = jnp.arange(count)

    def named(sizes, turn):
        used = int((sizes > 0).sum())
        fixed = max(1, used // 4)
        shifted = fixed + (places - fixed + turn * (used - fixed)) % max(1, count - fixed)
        return jnp.zeros((count,), jnp.int32).at[sequence[jnp.where(places < fixed, places, shifted)]].set(jnp.asarray(sizes, jnp.int32))

    sizes = jnp.where(number % 4 == 0, named(crowded, number // 4), named(ordinary, number - number // 4 - 1))
    mixed = jax.random.permutation(jax.random.fold_in(own, 3), count)
    donor, receiver = mixed[0:count // 2 * 2:2], mixed[1:count // 2 * 2:2]
    slack = jnp.minimum(sizes[donor] - 1, most - sizes[receiver]) // 2
    slack = jnp.where((donor == sequence[0]) | (receiver == sequence[0]) | (sizes[receiver] == 0), 0, jnp.maximum(slack, 0))
    shifted = jax.random.randint(jax.random.fold_in(own, 4), (count // 2,), 0, 1 << 20) % (slack + 1)
    sizes = sizes.at[donor].add(-shifted).at[receiver].add(shifted)
    items = jnp.searchsorted(jnp.cumsum(sizes), jnp.arange(rows * top), side="right").astype(jnp.int32)
    table = items.reshape(top, rows).T
    table = table[jax.random.permutation(jax.random.fold_in(own, 1), rows)]
    turn = jax.random.randint(jax.random.fold_in(own, 2), (rows, 1), 0, top)
    return jnp.take_along_axis(table, (jnp.arange(top)[None, :] + turn) % top, axis=1)


def portions_of(number_of, total, most, slope, full):
    portions = [(1 << 20) // math.isqrt(rank ** slope) + 1 for rank in range(1, number_of + 1)]
    largest = most if full else min(most, max(-(-total // number_of), total * portions[0] // sum(portions)))
    least = 1 if total - largest >= number_of - 1 else 0
    given, rest = [largest] + [least] * (number_of - 1), total - largest - least * (number_of - 1)
    while rest > 0:
        movable = [i for i in range(1, number_of) if given[i] < largest] or [i for i in range(1, number_of) if given[i] < most]
        whole, budget = sum([portions[i] for i in movable]), rest
        for i in movable:
            more = min(most - given[i], max(1, budget * portions[i] // whole), rest)
            given[i] = given[i] + more
            rest = rest - more
    return np.array(given)


def scatter_about(rng, dims, deviation, bound, cuts=(), held_as=jnp.bfloat16):
    drawn = jax.random.normal(rng, dims, jnp.float32) * deviation
    if len(cuts) > 0:
        drawn = shard_levels(rng, dims, cuts, -0.22, 0.18) * drawn
    return jnp.clip(drawn, min=-bound, max=bound).astype(held_as)


def setup_inputs(seed: int = 0) -> dict:
    arg_keys = jax.random.split(jax.random.key(seed), 13)
    attn_out = scatter_about(arg_keys[0], (TOKENS, HD), 1.0, 6.0, ((0, 256),))
    resid = scatter_about(arg_keys[1], (TOKENS, D), 1.0, 6.0, ((0, 256),))
    w_o = scatter_about(arg_keys[2], (HD, D), HD ** -0.5, 0.15625)
    norm1_gain = jnp.clip(1.0 + 0.18 * jax.random.normal(arg_keys[3], (D,), jnp.float32), 0.1, 1.9)
    router_w = draw_router_w(jax.random.fold_in(arg_keys[12], 71), 0)
    route_slot_keys = jax.random.split(jax.random.fold_in(arg_keys[5], 1), TOKENS // ROWS_DEV)
    route_slot_turns = jax.random.permutation(jax.random.fold_in(arg_keys[5], 3), TOKENS // ROWS_DEV)
    route_slot = jax.vmap(lambda own, number: routed_block(jax.random.fold_in(arg_keys[5], 2), own, number, ROWS_DEV, SLOTS, TOP, CAP, 2))(route_slot_keys, route_slot_turns).reshape((TOKENS, TOP))
    slot_expert = draw_slot_expert(jax.random.fold_in(arg_keys[12], 71), 0)
    keep = with_ends((jax.random.randint(arg_keys[7], (TOKENS,), 0, 8) < 7).astype(jnp.int32), jax.random.fold_in(arg_keys[7], 1), 0, 1)
    w_gate = scatter_about(arg_keys[8], (SLOTS, D, FF), D ** -0.5, 0.15625, ((0, 32), (1, 8)))
    w_up = scatter_about(arg_keys[9], (SLOTS, D, FF), D ** -0.5, 0.15625, ((0, 32), (1, 8)))
    w_down = scatter_about(arg_keys[10], (SLOTS, D, FF), FF ** -0.5, 0.25, ((0, 32), (1, 8)))
    norm2_gain = jnp.clip(1.0 + 0.18 * jax.random.normal(arg_keys[11], (D,), jnp.float32), 0.1, 1.9)
    return {"attn_out": attn_out, "resid": resid, "w_o": w_o, "norm1_gain": norm1_gain, "router_w": router_w, "route_slot": route_slot, "slot_expert": slot_expert, "keep": keep, "w_gate": w_gate, "w_up": w_up, "w_down": w_down, "norm2_gain": norm2_gain}


eps = 1e-05

def rms_scale(values, gain):
    mean_sq = lax.optimization_barrier(jnp.mean(values * values, axis=-1, keepdims=True))
    return values * lax.rsqrt(mean_sq + eps) * gain

def reference(attn_out, resid, w_o, norm1_gain, router_w, route_slot, slot_expert, keep, w_gate, w_up, w_down, norm2_gain):
    hidden_state = resid.astype(jnp.float32) + jnp.dot(attn_out, w_o, preferred_element_type=jnp.float32)
    normed = rms_scale(hidden_state, norm1_gain).astype(jnp.bfloat16)
    logits = jnp.dot(normed.astype(jnp.float32), router_w, precision=lax.Precision.HIGHEST)
    expert_of = slot_expert[route_slot]
    probs = jax.nn.softmax(jnp.take_along_axis(logits, expert_of, axis=1), axis=-1)
    live_rows = keep > 0
    weight = (probs * live_rows[:, None].astype(jnp.float32)).reshape(-1)
    flat_slot = route_slot.reshape(-1)
    live = jnp.repeat(live_rows, TOP)
    limit = CAP * (TOKENS // ROWS_DEV)

    def one_slot(total, slot):
        hit = (flat_slot == slot) & live
        index = jnp.nonzero(hit, size=limit, fill_value=0)[0]
        valid = jnp.arange(limit) < jnp.sum(hit.astype(jnp.int32))
        token_index = index // TOP
        rows = normed[token_index]
        gate = jnp.dot(rows, w_gate[slot], preferred_element_type=jnp.float32)
        up = jnp.dot(rows, w_up[slot], preferred_element_type=jnp.float32)
        act = (jax.nn.silu(gate) * up).astype(jnp.bfloat16)
        expert_y = jnp.dot(act, w_down[slot].T, preferred_element_type=jnp.float32).astype(jnp.bfloat16)
        scale = jnp.where(valid, weight[index], jnp.float32(0.0))
        total = total.at[token_index].add(scale[:, None] * expert_y.astype(jnp.float32))
        return (total, None)
    start = jnp.zeros(hidden_state.shape, jnp.float32)
    moe, unused = lax.scan(one_slot, start, jnp.arange(SLOTS, dtype=jnp.int32))
    mixed = hidden_state + moe
    return rms_scale(mixed, norm2_gain).astype(jnp.bfloat16)
```

```python
import functools

import jax
import jax.numpy as jnp
from jax import lax
from jax.experimental import pallas as pl
from jax.experimental.pallas import tpu as pltpu
from jax.sharding import Mesh
from jax.sharding import PartitionSpec as P

EPS = 1e-05
D = 1536
FF = 512
TOP = 8
SLOTS = 64
ROWS = 128
CAP = 32
BLOCKS = 16
LOCAL = 4
CHUNK = D // 8
GROUP = 2 * CHUNK
F32 = jnp.float32
BF16 = jnp.bfloat16
VMEM_LIMIT = 56 * 1024 * 1024


def params(*semantics):
    return pltpu.CompilerParams(
        dimension_semantics=semantics or None, vmem_limit_bytes=VMEM_LIMIT
    )


def entry_kernel(
    attn_ref, resid_ref, wo_ref, gain_ref, router_ref, route_ref, expert_ref, keep_ref,
    hidden_ref, normed_ref, weight_ref,
):
    step = pl.program_id(0)
    width = wo_ref.shape[1]
    cols = pl.ds(step * width, width)
    hidden_ref[:, cols] = resid_ref[...].astype(F32) + jnp.dot(
        attn_ref[...], wo_ref[...], preferred_element_type=F32
    )

    @pl.when(step == pl.num_programs(0) - 1)
    def _():
        values = hidden_ref[...]
        mean_sq = jnp.mean(values * values, axis=-1, keepdims=True)
        normed = (values * lax.rsqrt(mean_sq + EPS) * gain_ref[...]).astype(BF16)
        normed_ref[...] = normed
        logits = jnp.dot(
            normed.astype(F32), router_ref[...], precision=lax.Precision.HIGHEST,
            preferred_element_type=F32,
        )
        experts = logits.shape[1]
        lanes = 128
        pick = lax.broadcasted_iota(jnp.int32, (experts, lanes), 0) == expert_ref[...]
        by_slot = jnp.dot(
            logits, pick.astype(F32), precision=lax.Precision.HIGHEST,
            preferred_element_type=F32,
        )
        slot = lax.broadcasted_iota(jnp.int32, (ROWS, lanes), 1)
        named = slot == route_ref[:, 0:1]
        for k in range(1, TOP):
            named = named | (slot == route_ref[:, k : k + 1])
        top = jnp.max(jnp.where(named, by_slot, -jnp.inf), axis=-1, keepdims=True)
        grown = jnp.where(named, jnp.exp(jnp.where(named, by_slot - top, 0.0)), 0.0)
        probs = grown / jnp.sum(grown, axis=-1, keepdims=True)
        live = jnp.where(keep_ref[...] > 0, probs, 0.0)
        weight_ref[...] = jnp.transpose(live)[:SLOTS]


def entry(attn_out, resid, w_o, gain, router_w, route_slot, slot_expert, keep):
    steps = 6
    width = D // steps
    whole = lambda shape: pl.BlockSpec(shape, lambda i: (0, 0))
    return pl.pallas_call(
        entry_kernel,
        grid=(steps,),
        in_specs=[
            whole((ROWS, D)),
            pl.BlockSpec((ROWS, width), lambda i: (0, i)),
            pl.BlockSpec((D, width), lambda i: (0, i)),
            whole((1, D)),
            whole(router_w.shape),
            whole((ROWS, TOP)),
            whole((1, 128)),
            whole((ROWS, 1)),
        ],
        out_specs=[whole((ROWS, D)), whole((ROWS, D)), whole((SLOTS, ROWS))],
        out_shape=[
            jax.ShapeDtypeStruct((ROWS, D), F32),
            jax.ShapeDtypeStruct((ROWS, D), BF16),
            jax.ShapeDtypeStruct((SLOTS, ROWS), F32),
        ],
        compiler_params=params("arbitrary"),
        name="entry",
    )(attn_out, resid, w_o, gain, router_w, route_slot, slot_expert, keep)


def compact_kernel(weight_ref, rows_ref, packed_ref, spread_ref, scale_ref):
    weight = weight_ref[0]
    hit = weight > 0.0
    earlier = (
        lax.broadcasted_iota(jnp.int32, (ROWS, ROWS), 0)
        < lax.broadcasted_iota(jnp.int32, (ROWS, ROWS), 1)
    ).astype(BF16)
    place = jnp.dot(hit.astype(BF16), earlier, preferred_element_type=F32)
    place = jnp.where(hit, place, -1.0)
    rank = lax.broadcasted_iota(jnp.int32, (CAP, ROWS), 0).astype(F32)
    picks = [rank == place[s : s + 1] for s in range(LOCAL)]
    scale_ref[:, 0] = jnp.stack(
        [
            jnp.sum(jnp.where(picks[s], weight[s : s + 1], 0.0), axis=1, keepdims=True)
            for s in range(LOCAL)
        ]
    )
    pick = jnp.concatenate([p.astype(F32) for p in picks], axis=0)
    spread_ref[0] = jnp.transpose(pick).astype(BF16)
    packed = jnp.dot(pick.astype(BF16), rows_ref[0], preferred_element_type=F32).astype(BF16)
    packed_ref[:, 0] = packed.reshape(LOCAL, CAP, D)


def compact(weight, rows):
    return pl.pallas_call(
        compact_kernel,
        grid=(BLOCKS,),
        in_specs=[
            pl.BlockSpec((1, LOCAL, ROWS), lambda b: (b, 0, 0)),
            pl.BlockSpec((1, ROWS, D), lambda b: (b, 0, 0)),
        ],
        out_specs=[
            pl.BlockSpec((LOCAL, 1, CAP, D), lambda b: (0, b, 0, 0)),
            pl.BlockSpec((1, ROWS, LOCAL * CAP), lambda b: (b, 0, 0)),
            pl.BlockSpec((LOCAL, 1, CAP, 1), lambda b: (0, b, 0, 0)),
        ],
        out_shape=[
            jax.ShapeDtypeStruct((LOCAL, BLOCKS, CAP, D), BF16),
            jax.ShapeDtypeStruct((BLOCKS, ROWS, LOCAL * CAP), BF16),
            jax.ShapeDtypeStruct((LOCAL, BLOCKS, CAP, 1), F32),
        ],
        compiler_params=params("arbitrary"),
        name="compact",
    )(weight, rows)


def hidden_units_kernel(packed_ref, gate_ref, up_ref, act_ref):
    rows = packed_ref[0].reshape(BLOCKS * CAP, D)
    gate = jnp.dot(rows, gate_ref[...].reshape(D, FF), preferred_element_type=F32)
    up = jnp.dot(rows, up_ref[...].reshape(D, FF), preferred_element_type=F32)
    act_ref[0] = (gate / (1.0 + jnp.exp(-gate)) * up).astype(BF16)


def hidden_units(packed, weights):
    def block(which):
        return pl.BlockSpec((1, 8, 1, 1, CHUNK, FF), lambda s: (s // 2, 0, which, s % 2, 0, 0))

    return pl.pallas_call(
        hidden_units_kernel,
        grid=(LOCAL,),
        in_specs=[pl.BlockSpec((1, BLOCKS, CAP, D), lambda s: (s, 0, 0, 0)), block(0), block(1)],
        out_specs=pl.BlockSpec((1, BLOCKS * CAP, FF), lambda s: (s, 0, 0)),
        out_shape=jax.ShapeDtypeStruct((LOCAL, BLOCKS * CAP, FF), BF16),
        compiler_params=params("arbitrary"),
        name="hidden_units",
    )(packed, weights, weights)


def spread_kernel(order_ref, act_ref, down_ref, scale_ref, spread_ref, send_ref, keep_ref, part_ref):
    for s in range(LOCAL):
        down = down_ref[s // 2, :, 0, s % 2].reshape(GROUP, FF)
        part = lax.dot_general(
            act_ref[s], down, (((1,), (1,)), ((), ())), preferred_element_type=F32
        )
        scale = scale_ref[s].reshape(BLOCKS * CAP, 1)
        part_ref[:, s] = (part * scale).astype(BF16).reshape(BLOCKS, CAP, GROUP)
    half = BLOCKS // 2
    for j in range(BLOCKS):
        b = order_ref[j]
        rows = part_ref[b].reshape(LOCAL * CAP, GROUP)
        out = jnp.dot(spread_ref[b], rows, preferred_element_type=F32).astype(BF16)
        if j < half:
            keep_ref[j] = out
        else:
            send_ref[j - half] = out


def spread_rows(order, act, weights, scale, spread, group):
    half = BLOCKS // 2
    full = lambda shape: pl.BlockSpec(shape, lambda i, o: (0,) * len(shape))
    return pl.pallas_call(
        spread_kernel,
        grid_spec=pltpu.PrefetchScalarGridSpec(
            num_scalar_prefetch=1,
            grid=(1,),
            in_specs=[
                full(act.shape),
                pl.BlockSpec((2, 2, 1, 2, CHUNK, FF), lambda i, o: (0, group, 2, 0, 0, 0)),
                full(scale.shape),
                full(spread.shape),
            ],
            out_specs=[full((half, ROWS, GROUP)), full((half, ROWS, GROUP))],
            scratch_shapes=[pltpu.VMEM((BLOCKS, LOCAL, CAP, GROUP), BF16)],
        ),
        out_shape=[jax.ShapeDtypeStruct((half, ROWS, GROUP), BF16)] * 2,
        compiler_params=params("arbitrary"),
        name="spread",
    )(order, act, weights, scale, spread)


def closing_kernel(hidden_ref, gain_ref, *refs):
    pairs, out_ref = refs[:-1], refs[-1]
    moe = jnp.concatenate(
        [
            pairs[2 * g][...].astype(F32) + pairs[2 * g + 1][...].astype(F32)
            for g in range(len(pairs) // 2)
        ],
        axis=1,
    )
    mixed = hidden_ref[...] + moe
    mean_sq = jnp.mean(mixed * mixed, axis=-1, keepdims=True)
    out_ref[...] = (mixed * lax.rsqrt(mean_sq + EPS) * gain_ref[...]).astype(BF16)


def closing(hidden, gain, pairs):
    return pl.pallas_call(
        closing_kernel,
        out_shape=jax.ShapeDtypeStruct((ROWS, D), BF16),
        compiler_params=params(),
        name="closing",
    )(hidden, gain, *pairs)


def near(i):
    return i ^ 1


def far(i):
    return 3 - i


def reach(first, i):
    other = far if first is near else near
    return [i, other(i), first(i), other(first(i))]


def links(turn):
    return [(i, turn(i)) for i in range(4)]


def add(a, b):
    return (a.astype(F32) + b.astype(F32)).astype(BF16)


def body(
    attn_out, resid, w_o, norm1_gain, router_w, route_slot, slot_expert, keep,
    w_gate, w_up, w_down, norm2_gain,
):
    joined = jnp.stack([w_gate, w_up, w_down])
    weights = lax.all_gather(joined, ("core", "blk"), axis=0, tiled=False)
    weights = weights.reshape(2, 8, 3, 2, CHUNK, FF)

    slot_row = jnp.full((1, 128), -1, jnp.int32).at[0, :SLOTS].set(slot_expert)
    hidden, normed, weight = entry(
        attn_out, resid, w_o, norm1_gain.reshape(1, D), router_w, route_slot, slot_row,
        keep.reshape(ROWS, 1),
    )
    plane = ("x", "y")
    weight = lax.all_to_all(
        weight.reshape(BLOCKS, LOCAL, ROWS), plane, split_axis=0, concat_axis=0, tiled=True
    )
    copies = jnp.broadcast_to(normed[None], (BLOCKS, ROWS, D))
    rows = lax.all_to_all(copies, plane, split_axis=0, concat_axis=0, tiled=True)
    packed, spread, scale = compact(weight, rows)
    act = hidden_units(packed, weights)

    x, y = lax.axis_index("x"), lax.axis_index("y")
    plans = [("x", near), ("x", far), ("y", near), ("y", far)]
    pairs = []
    for group, (axis, first) in enumerate(plans):
        if axis == "x":
            second_axis = "y"
            order = [4 * a + b for a in reach(first, x) for b in reach(first, y)]
        else:
            second_axis = "x"
            order = [4 * b + a for a in reach(first, y) for b in reach(first, x)]
        order = jnp.stack(order).astype(jnp.int32)
        send, kept = spread_rows(order, act, weights, scale, spread, group)
        other = far if first is near else near
        got = lax.ppermute(send, axis, links(first))
        send, kept = add(kept[4:], got[4:]), add(kept[:4], got[:4])
        got = lax.ppermute(send, axis, links(other))
        send, kept = add(kept[2:], got[2:]), add(kept[:2], got[:2])
        got = lax.ppermute(send, second_axis, links(first))
        send, kept = add(kept[1], got[1]), add(kept[0], got[0])
        got = lax.ppermute(send, second_axis, links(other))
        pairs += [kept, got]
    return closing(hidden, norm2_gain.reshape(1, D), pairs)


def solution(mesh):
    fine = Mesh(mesh.devices.reshape(4, 4, 2, 8), ("x", "y", "core", "blk"))
    rows = P(("x", "y", "core", "blk"), None)
    slots = P(("x", "y", "core"), "blk", None)
    placed = (
        rows, rows, P(), P(), P(), rows, P(), P(("x", "y", "core", "blk")),
        slots, slots, slots, P(),
    )
    return jax.shard_map(body, mesh=fine, in_specs=placed, out_specs=rows, check_vma=False)
```

```python
import functools

import jax
import jax.numpy as jnp
from jax import lax
from jax.experimental import pallas as pl
from jax.experimental.pallas import tpu as pltpu
from jax.sharding import Mesh
from jax.sharding import PartitionSpec as P

EPS = 1e-05
D = 1536
FF = 512
TOP = 8
SLOTS = 64
ROWS = 128
CAP = 32
BLOCKS = 16
LOCAL = 4
CHUNK = D // 8
GROUP = 2 * CHUNK
F32 = jnp.float32
BF16 = jnp.bfloat16
MIB = 1024 * 1024


def params(mib, *semantics):
    return pltpu.CompilerParams(
        dimension_semantics=semantics or None, vmem_limit_bytes=mib * MIB
    )


PLANS = (("x", "y", 1, 3), ("x", "y", 3, 1), ("y", "x", 1, 3), ("y", "x", 3, 1))


def block_at(plan, x, y, j):
    big, small, first, other = plan
    bit = lambda n: (j >> n) & 1
    low = bit(0) * other ^ bit(1) * first
    high = bit(2) * other ^ bit(3) * first
    if big == "x":
        return 4 * (x ^ high) + (y ^ low)
    return 4 * (x ^ low) + (y ^ high)


def each(count, unroll, step):
    def run(i, carry):
        step(i)
        return carry

    lax.fori_loop(0, count, run, 0, unroll=unroll)


def links(turn):
    return [(i, i ^ turn) for i in range(4)]


def gather_plane(own, plan):
    big, small, first, other = plan
    held = own[None]
    for axis, turn in ((small, other), (small, first), (big, other)):
        held = jnp.concatenate([held, lax.ppermute(held, axis, links(turn))])
    return held, lax.ppermute(held, big, links(first))


def entry_kernel(
    attn_ref, resid_ref, wo_ref, gain_ref, router_ref, route_ref, expert_ref, keep_ref,
    hidden_ref, normed_ref, weight_ref,
):
    step = pl.program_id(0)
    width = wo_ref.shape[1]
    cols = pl.ds(step * width, width)
    hidden_ref[:, cols] = resid_ref[...].astype(F32) + jnp.dot(
        attn_ref[...], wo_ref[...], preferred_element_type=F32
    )

    @pl.when(step == pl.num_programs(0) - 1)
    def _():
        values = hidden_ref[...]
        mean_sq = jnp.mean(values * values, axis=-1, keepdims=True)
        normed = (values * lax.rsqrt(mean_sq + EPS) * gain_ref[...]).astype(BF16)
        for group in range(len(PLANS)):
            normed_ref[group] = normed[:, group * GROUP : (group + 1) * GROUP]
        logits = jnp.dot(
            normed.astype(F32), router_ref[...], precision=lax.Precision.HIGHEST,
            preferred_element_type=F32,
        )
        experts = logits.shape[1]
        lanes = 128
        pick = lax.broadcasted_iota(jnp.int32, (experts, lanes), 0) == expert_ref[...]
        by_slot = jnp.dot(
            logits, pick.astype(F32), precision=lax.Precision.HIGHEST,
            preferred_element_type=F32,
        )
        slot = lax.broadcasted_iota(jnp.int32, (ROWS, lanes), 1)
        named = slot == route_ref[:, 0:1]
        for k in range(1, TOP):
            named = named | (slot == route_ref[:, k : k + 1])
        top = jnp.max(jnp.where(named, by_slot, -jnp.inf), axis=-1, keepdims=True)
        grown = jnp.where(named, jnp.exp(jnp.where(named, by_slot - top, 0.0)), 0.0)
        probs = grown / jnp.sum(grown, axis=-1, keepdims=True)
        live = jnp.where(keep_ref[...] > 0, probs, 0.0)
        weight_ref[...] = jnp.transpose(live)[:SLOTS]


def entry(attn_out, resid, w_o, gain, router_w, route_slot, slot_expert, keep):
    steps = 6
    width = D // steps
    whole = lambda shape: pl.BlockSpec(shape, lambda i: (0, 0))
    return pl.pallas_call(
        entry_kernel,
        grid=(steps,),
        in_specs=[
            whole((ROWS, D)),
            pl.BlockSpec((ROWS, width), lambda i: (0, i)),
            pl.BlockSpec((D, width), lambda i: (0, i)),
            whole((1, D)),
            whole(router_w.shape),
            whole((ROWS, TOP)),
            whole((1, 128)),
            whole((ROWS, 1)),
        ],
        out_specs=[
            whole((ROWS, D)),
            pl.BlockSpec((len(PLANS), ROWS, GROUP), lambda i: (0, 0, 0)),
            whole((SLOTS, ROWS)),
        ],
        out_shape=[
            jax.ShapeDtypeStruct((ROWS, D), F32),
            jax.ShapeDtypeStruct((len(PLANS), ROWS, GROUP), BF16),
            jax.ShapeDtypeStruct((SLOTS, ROWS), F32),
        ],
        compiler_params=params(16, "arbitrary"),
        name="entry",
    )(attn_out, resid, w_o, gain, router_w, route_slot, slot_expert, keep)


def compact_kernel(place_ref, *refs):
    weight_refs, row_refs = refs[:2], refs[2:10]
    packed_ref, spread_ref, scale_ref, pick_ref = refs[10:]
    x, y = place_ref[0], place_ref[1]
    half = BLOCKS // 2
    earlier = (
        lax.broadcasted_iota(jnp.int32, (ROWS, ROWS), 0)
        < lax.broadcasted_iota(jnp.int32, (ROWS, ROWS), 1)
    ).astype(BF16)
    rank = lax.broadcasted_iota(jnp.int32, (CAP, ROWS), 0).astype(F32)
    def choose(ref, start, i):
        b = block_at(PLANS[0], x, y, start + i)
        weight = ref[i, 4 * x + y]
        hit = weight > 0.0
        place = jnp.dot(hit.astype(BF16), earlier, preferred_element_type=F32)
        place = jnp.where(hit, place, -1.0)
        picks = [rank == place[s : s + 1] for s in range(LOCAL)]
        for s in range(LOCAL):
            scale_ref[s, b] = jnp.sum(
                jnp.where(picks[s], weight[s : s + 1], 0.0), axis=1, keepdims=True
            )
        pick = jnp.concatenate([p.astype(F32) for p in picks], axis=0)
        spread_ref[b] = jnp.transpose(pick).astype(BF16)
        pick_ref[b] = pick.astype(BF16)

    def pack(ref, group, start, i):
        b = block_at(PLANS[group], x, y, start + i)
        packed = jnp.dot(pick_ref[b], ref[i], preferred_element_type=F32).astype(BF16)
        packed_ref[:, b, :, group * GROUP : (group + 1) * GROUP] = packed.reshape(
            LOCAL, CAP, GROUP
        )

    for n, ref in enumerate(weight_refs):
        each(half, 2, functools.partial(choose, ref, n * half))
    for n, ref in enumerate(row_refs):
        each(half, 4, functools.partial(pack, ref, n // 2, n % 2 * half))


def compact(place, weights, rows):
    vmem = pl.BlockSpec(memory_space=pltpu.VMEM)
    return pl.pallas_call(
        compact_kernel,
        in_specs=[pl.BlockSpec(memory_space=pltpu.SMEM)] + [vmem] * 10,
        out_specs=[vmem] * 3,
        out_shape=[
            jax.ShapeDtypeStruct((LOCAL, BLOCKS, CAP, D), BF16),
            jax.ShapeDtypeStruct((BLOCKS, ROWS, LOCAL * CAP), BF16),
            jax.ShapeDtypeStruct((LOCAL, BLOCKS, CAP, 1), F32),
        ],
        scratch_shapes=[pltpu.VMEM((BLOCKS, LOCAL * CAP, ROWS), BF16)],
        compiler_params=params(24),
        name="compact",
    )(place, *weights, *rows)


def hidden_units_kernel(packed_ref, gate_ref, up_ref, act_ref):
    rows = packed_ref[0].reshape(BLOCKS * CAP, D)
    gate = jnp.dot(rows, gate_ref[...].reshape(D, FF), preferred_element_type=F32)
    up = jnp.dot(rows, up_ref[...].reshape(D, FF), preferred_element_type=F32)
    act_ref[0] = (gate / (1.0 + jnp.exp(-gate)) * up).astype(BF16)


def hidden_units(packed, weights):
    def block(which):
        return pl.BlockSpec((1, 8, 1, 1, CHUNK, FF), lambda s: (s // 2, 0, which, s % 2, 0, 0))

    return pl.pallas_call(
        hidden_units_kernel,
        grid=(LOCAL,),
        in_specs=[pl.BlockSpec((1, BLOCKS, CAP, D), lambda s: (s, 0, 0, 0)), block(0), block(1)],
        out_specs=pl.BlockSpec((1, BLOCKS * CAP, FF), lambda s: (s, 0, 0)),
        out_shape=jax.ShapeDtypeStruct((LOCAL, BLOCKS * CAP, FF), BF16),
        compiler_params=params(24, "arbitrary"),
        name="hidden_units",
    )(packed, weights, weights)


def spread_kernel(plan, place_ref, act_ref, down_ref, scale_ref, spread_ref, send_ref, keep_ref, part_ref):
    for s in range(LOCAL):
        down = down_ref[s // 2, :, 0, s % 2].reshape(GROUP, FF)
        part = lax.dot_general(
            act_ref[s], down, (((1,), (1,)), ((), ())), preferred_element_type=F32
        )
        scale = scale_ref[s].reshape(BLOCKS * CAP, 1)
        part_ref[:, s] = (part * scale).astype(BF16).reshape(BLOCKS, CAP, GROUP)
    half = BLOCKS // 2

    def back(out_ref, start, i):
        b = block_at(plan, place_ref[0], place_ref[1], start + i)
        rows = part_ref[b].reshape(LOCAL * CAP, GROUP)
        out_ref[i] = jnp.dot(spread_ref[b], rows, preferred_element_type=F32).astype(BF16)

    each(half, 4, functools.partial(back, keep_ref, 0))
    each(half, 4, functools.partial(back, send_ref, half))


def spread_rows(place, act, weights, scale, spread, group):
    half = BLOCKS // 2
    full = lambda shape: pl.BlockSpec(shape, lambda i, o: (0,) * len(shape))
    return pl.pallas_call(
        functools.partial(spread_kernel, PLANS[group]),
        grid_spec=pltpu.PrefetchScalarGridSpec(
            num_scalar_prefetch=1,
            grid=(1,),
            in_specs=[
                full(act.shape),
                pl.BlockSpec((2, 2, 1, 2, CHUNK, FF), lambda i, o: (0, group, 2, 0, 0, 0)),
                full(scale.shape),
                full(spread.shape),
            ],
            out_specs=[full((half, ROWS, GROUP)), full((half, ROWS, GROUP))],
            scratch_shapes=[pltpu.VMEM((BLOCKS, LOCAL, CAP, GROUP), BF16)],
        ),
        out_shape=[jax.ShapeDtypeStruct((half, ROWS, GROUP), BF16)] * 2,
        compiler_params=params(24, "arbitrary"),
        name="spread",
    )(place, act, weights, scale, spread)


def closing_kernel(hidden_ref, gain_ref, *refs):
    pairs, out_ref = refs[:-1], refs[-1]
    moe = jnp.concatenate(
        [
            pairs[2 * g][...].astype(F32) + pairs[2 * g + 1][...].astype(F32)
            for g in range(len(pairs) // 2)
        ],
        axis=1,
    )
    mixed = hidden_ref[...] + moe
    mean_sq = jnp.mean(mixed * mixed, axis=-1, keepdims=True)
    out_ref[...] = (mixed * lax.rsqrt(mean_sq + EPS) * gain_ref[...]).astype(BF16)


def closing(hidden, gain, pairs):
    return pl.pallas_call(
        closing_kernel,
        out_shape=jax.ShapeDtypeStruct((ROWS, D), BF16),
        compiler_params=params(8),
        name="closing",
    )(hidden, gain, *pairs)


def add(a, b):
    return (a.astype(F32) + b.astype(F32)).astype(BF16)


def body(
    attn_out, resid, w_o, norm1_gain, router_w, route_slot, slot_expert, keep,
    w_gate, w_up, w_down, norm2_gain,
):
    joined = jnp.stack([w_gate, w_up, w_down])
    weights = lax.all_gather(joined, ("core", "blk"), axis=0, tiled=False)
    weights = weights.reshape(2, 8, 3, 2, CHUNK, FF)

    slot_row = jnp.full((1, 128), -1, jnp.int32).at[0, :SLOTS].set(slot_expert)
    hidden, normed, weight = entry(
        attn_out, resid, w_o, norm1_gain.reshape(1, D), router_w, route_slot, slot_row,
        keep.reshape(ROWS, 1),
    )
    place = jnp.stack([lax.axis_index("x"), lax.axis_index("y")]).astype(jnp.int32)
    slot_weights = gather_plane(weight.reshape(BLOCKS, LOCAL, ROWS), PLANS[0])
    rows = []
    for group, plan in enumerate(PLANS):
        rows += gather_plane(normed[group], plan)
    packed, spread, scale = compact(place, slot_weights, rows)
    act = hidden_units(packed, weights)

    pairs = []
    for group, (big, small, first, other) in enumerate(PLANS):
        send, kept = spread_rows(place, act, weights, scale, spread, group)
        got = lax.ppermute(send, big, links(first))
        send, kept = add(kept[4:], got[4:]), add(kept[:4], got[:4])
        got = lax.ppermute(send, big, links(other))
        send, kept = add(kept[2:], got[2:]), add(kept[:2], got[:2])
        got = lax.ppermute(send, small, links(first))
        send, kept = add(kept[1], got[1]), add(kept[0], got[0])
        got = lax.ppermute(send, small, links(other))
        pairs += [kept, got]
    return closing(hidden, norm2_gain.reshape(1, D), pairs)


def solution(mesh):
    fine = Mesh(mesh.devices.reshape(4, 4, 2, 8), ("x", "y", "core", "blk"))
    rows = P(("x", "y", "core", "blk"), None)
    slots = P(("x", "y", "core"), "blk", None)
    placed = (
        rows, rows, P(), P(), P(), rows, P(), P(("x", "y", "core", "blk")),
        slots, slots, slots, P(),
    )
    return jax.shard_map(body, mesh=fine, in_specs=placed, out_specs=rows, check_vma=False)
```

```python
import functools

import jax
import jax.numpy as jnp
from jax import lax
from jax.experimental import pallas as pl
from jax.experimental.pallas import tpu as pltpu
from jax.sharding import Mesh
from jax.sharding import PartitionSpec as P

EPS = 1e-05
D = 1536
FF = 512
TOP = 8
SLOTS = 64
ROWS = 128
CAP = 32
BLOCKS = 16
LOCAL = 4
CHUNK = D // 8
GROUP = 2 * CHUNK
F32 = jnp.float32
BF16 = jnp.bfloat16
MIB = 1024 * 1024


def params(mib, *semantics):
    return pltpu.CompilerParams(
        dimension_semantics=semantics or None, vmem_limit_bytes=mib * MIB
    )


PLANS = (("x", "y", 1, 3), ("x", "y", 3, 1), ("y", "x", 1, 3), ("y", "x", 3, 1))


def block_at(plan, x, y, j):
    big, small, first, other = plan
    bit = lambda n: (j >> n) & 1
    low = bit(0) * other ^ bit(1) * first
    high = bit(2) * other ^ bit(3) * first
    if big == "x":
        return 4 * (x ^ high) + (y ^ low)
    return 4 * (x ^ low) + (y ^ high)


def each(count, unroll, step):
    def run(i, carry):
        step(i)
        return carry

    lax.fori_loop(0, count, run, 0, unroll=unroll)


def links(turn):
    return [(i, i ^ turn) for i in range(4)]


def gather_plane(own, plan):
    big, small, first, other = plan
    held = own[None]
    for axis, turn in ((small, other), (small, first), (big, other)):
        held = jnp.concatenate([held, lax.ppermute(held, axis, links(turn))])
    return held, lax.ppermute(held, big, links(first))


def entry_kernel(
    attn_ref, resid_ref, wo_ref, gain_ref, router_ref, route_ref, expert_ref, keep_ref,
    hidden_ref, normed_ref, weight_ref,
):
    step = pl.program_id(0)
    width = wo_ref.shape[1]
    cols = pl.ds(step * width, width)
    hidden_ref[:, cols] = resid_ref[...].astype(F32) + jnp.dot(
        attn_ref[...], wo_ref[...], preferred_element_type=F32
    )

    @pl.when(step == pl.num_programs(0) - 1)
    def _():
        values = hidden_ref[...]
        mean_sq = jnp.mean(values * values, axis=-1, keepdims=True)
        normed = (values * lax.rsqrt(mean_sq + EPS) * gain_ref[...]).astype(BF16)
        for group in range(len(PLANS)):
            normed_ref[group] = normed[:, group * GROUP : (group + 1) * GROUP]
        logits = jnp.dot(
            normed.astype(F32), router_ref[...], precision=lax.Precision.HIGHEST,
            preferred_element_type=F32,
        )
        experts = logits.shape[1]
        lanes = 128
        pick = lax.broadcasted_iota(jnp.int32, (experts, lanes), 0) == expert_ref[...]
        by_slot = jnp.dot(
            logits, pick.astype(F32), precision=lax.Precision.HIGHEST,
            preferred_element_type=F32,
        )
        slot = lax.broadcasted_iota(jnp.int32, (ROWS, lanes), 1)
        named = slot == route_ref[:, 0:1]
        for k in range(1, TOP):
            named = named | (slot == route_ref[:, k : k + 1])
        top = jnp.max(jnp.where(named, by_slot, -jnp.inf), axis=-1, keepdims=True)
        grown = jnp.where(named, jnp.exp(jnp.where(named, by_slot - top, 0.0)), 0.0)
        probs = grown / jnp.sum(grown, axis=-1, keepdims=True)
        live = jnp.where(keep_ref[...] > 0, probs, 0.0)
        weight_ref[...] = jnp.transpose(live)[:SLOTS]


def entry(attn_out, resid, w_o, gain, router_w, route_slot, slot_expert, keep):
    steps = 6
    width = D // steps
    whole = lambda shape: pl.BlockSpec(shape, lambda i: (0, 0))
    return pl.pallas_call(
        entry_kernel,
        grid=(steps,),
        in_specs=[
            whole((ROWS, D)),
            pl.BlockSpec((ROWS, width), lambda i: (0, i)),
            pl.BlockSpec((D, width), lambda i: (0, i)),
            whole((1, D)),
            whole(router_w.shape),
            whole((ROWS, TOP)),
            whole((1, 128)),
            whole((ROWS, 1)),
        ],
        out_specs=[
            whole((ROWS, D)),
            pl.BlockSpec((len(PLANS), ROWS, GROUP), lambda i: (0, 0, 0)),
            whole((SLOTS, ROWS)),
        ],
        out_shape=[
            jax.ShapeDtypeStruct((ROWS, D), F32),
            jax.ShapeDtypeStruct((len(PLANS), ROWS, GROUP), BF16),
            jax.ShapeDtypeStruct((SLOTS, ROWS), F32),
        ],
        compiler_params=params(16, "arbitrary"),
        name="entry",
    )(attn_out, resid, w_o, gain, router_w, route_slot, slot_expert, keep)


def compact_kernel(place_ref, *refs):
    weight_refs, row_refs = refs[:2], refs[2:10]
    packed_ref, spread_ref, scale_ref, pick_ref = refs[10:]
    x, y = place_ref[0], place_ref[1]
    half = BLOCKS // 2
    earlier = (
        lax.broadcasted_iota(jnp.int32, (ROWS, ROWS), 0)
        < lax.broadcasted_iota(jnp.int32, (ROWS, ROWS), 1)
    ).astype(BF16)
    rank = lax.broadcasted_iota(jnp.int32, (CAP, ROWS), 0).astype(F32)
    def choose(ref, start, i):
        b = block_at(PLANS[0], x, y, start + i)
        weight = ref[i, 4 * x + y]
        hit = weight > 0.0
        place = jnp.dot(hit.astype(BF16), earlier, preferred_element_type=F32)
        place = jnp.where(hit, place, -1.0)
        picks = [rank == place[s : s + 1] for s in range(LOCAL)]
        for s in range(LOCAL):
            scale_ref[s, b] = jnp.sum(
                jnp.where(picks[s], weight[s : s + 1], 0.0), axis=1, keepdims=True
            )
        pick = jnp.concatenate([p.astype(F32) for p in picks], axis=0)
        spread_ref[b] = jnp.transpose(pick).astype(BF16)
        pick_ref[b] = pick.astype(BF16)

    def pack(ref, group, start, i):
        b = block_at(PLANS[group], x, y, start + i)
        packed = jnp.dot(pick_ref[b], ref[i], preferred_element_type=F32).astype(BF16)
        packed_ref[:, b, :, group * GROUP : (group + 1) * GROUP] = packed.reshape(
            LOCAL, CAP, GROUP
        )

    for n, ref in enumerate(weight_refs):
        each(half, 2, functools.partial(choose, ref, n * half))
    for n, ref in enumerate(row_refs):
        each(half, 4, functools.partial(pack, ref, n // 2, n % 2 * half))


def compact(place, weights, rows):
    vmem = pl.BlockSpec(memory_space=pltpu.VMEM)
    return pl.pallas_call(
        compact_kernel,
        in_specs=[pl.BlockSpec(memory_space=pltpu.SMEM)] + [vmem] * 10,
        out_specs=[vmem] * 3,
        out_shape=[
            jax.ShapeDtypeStruct((LOCAL, BLOCKS, CAP, D), BF16),
            jax.ShapeDtypeStruct((BLOCKS, ROWS, LOCAL * CAP), BF16),
            jax.ShapeDtypeStruct((LOCAL, BLOCKS, CAP, 1), F32),
        ],
        scratch_shapes=[pltpu.VMEM((BLOCKS, LOCAL * CAP, ROWS), BF16)],
        compiler_params=params(24),
        name="compact",
    )(place, *weights, *rows)


def hidden_units_kernel(packed_ref, gate_ref, up_ref, act_ref):
    rows = packed_ref[0].reshape(BLOCKS * CAP, D)
    gate = jnp.dot(rows, gate_ref[...].reshape(D, FF), preferred_element_type=F32)
    up = jnp.dot(rows, up_ref[...].reshape(D, FF), preferred_element_type=F32)
    act_ref[0] = (gate / (1.0 + jnp.exp(-gate)) * up).astype(BF16)


def hidden_units(packed, weights):
    def block(which):
        return pl.BlockSpec((1, 8, 1, 1, CHUNK, FF), lambda s: (s // 2, 0, which, s % 2, 0, 0))

    return pl.pallas_call(
        hidden_units_kernel,
        grid=(LOCAL,),
        in_specs=[pl.BlockSpec((1, BLOCKS, CAP, D), lambda s: (s, 0, 0, 0)), block(0), block(1)],
        out_specs=pl.BlockSpec((1, BLOCKS * CAP, FF), lambda s: (s, 0, 0)),
        out_shape=jax.ShapeDtypeStruct((LOCAL, BLOCKS * CAP, FF), BF16),
        compiler_params=params(24, "arbitrary"),
        name="hidden_units",
    )(packed, weights, weights)


def spread_kernel(plan, place_ref, act_ref, scale_ref, spread_ref, *refs):
    down_refs, (send_ref, keep_ref, part_ref) = refs[:-3], refs[-3:]
    x, y, core = place_ref[0], place_ref[1], place_ref[2]
    half = BLOCKS // 2
    for flip in range(2):
        for q in range(2):
            if len(down_refs) == 4:
                pieces = [down_refs[flip][q], down_refs[2 + flip][q]]
            else:
                pieces = [down_refs[0][2 * flip + q], down_refs[1][2 * (1 - flip) + q]]
            slot = 2 * (core ^ flip) + q
            part = lax.dot_general(
                act_ref[slot], jnp.concatenate(pieces), (((1,), (1,)), ((), ())),
                preferred_element_type=F32,
            )
            scale = scale_ref[slot].reshape(BLOCKS * CAP, 1)
            part_ref[:, slot] = (part * scale).astype(BF16).reshape(BLOCKS, CAP, GROUP)

    def back(out_ref, start, i):
        b = block_at(plan, x, y, start + i)
        rows = part_ref[b].reshape(LOCAL * CAP, GROUP)
        out_ref[i] = jnp.dot(spread_ref[b], rows, preferred_element_type=F32).astype(BF16)

    each(half, 4, functools.partial(back, keep_ref, 0))
    each(half, 4, functools.partial(back, send_ref, half))


def spread_rows(place, act, scale, spread, down, group):
    half = BLOCKS // 2
    vmem = pl.BlockSpec(memory_space=pltpu.VMEM)
    return pl.pallas_call(
        functools.partial(spread_kernel, PLANS[group]),
        in_specs=[pl.BlockSpec(memory_space=pltpu.SMEM)] + [vmem] * (3 + len(down)),
        out_specs=[vmem, vmem],
        scratch_shapes=[pltpu.VMEM((BLOCKS, LOCAL, CAP, GROUP), BF16)],
        out_shape=[jax.ShapeDtypeStruct((half, ROWS, GROUP), BF16)] * 2,
        compiler_params=params(16),
        name="spread",
    )(place, act, scale, spread, *down)


def closing_kernel(place_ref, hidden_ref, gain_ref, *refs):
    pairs, (out_ref, moe_ref) = refs[:-2], refs[-2:]
    core, z = place_ref[2], place_ref[3]
    step = 1 - 2 * core
    for g in range(len(pairs) // 2):
        total = pairs[2 * g][...].astype(F32) + pairs[2 * g + 1][...].astype(F32)
        ends = (z, z + 4) if g == 0 else (z - g * step, z + g * step)
        for n, end in enumerate(ends):
            moe_ref[end & 7] = total[:, n * CHUNK : (n + 1) * CHUNK]
    moe = jnp.concatenate([moe_ref[i] for i in range(8)], axis=1)
    mixed = hidden_ref[...] + moe
    mean_sq = jnp.mean(mixed * mixed, axis=-1, keepdims=True)
    out_ref[...] = (mixed * lax.rsqrt(mean_sq + EPS) * gain_ref[...]).astype(BF16)


def closing(place, hidden, gain, pairs):
    vmem = pl.BlockSpec(memory_space=pltpu.VMEM)
    return pl.pallas_call(
        closing_kernel,
        in_specs=[pl.BlockSpec(memory_space=pltpu.SMEM)] + [vmem] * (2 + len(pairs)),
        out_specs=vmem,
        out_shape=jax.ShapeDtypeStruct((ROWS, D), BF16),
        scratch_shapes=[pltpu.VMEM((8, ROWS, CHUNK), F32)],
        compiler_params=params(8),
        name="closing",
    )(place, hidden, gain, *pairs)


def down_groups(own):
    axes = ("core", "blk")
    swap = [(8 * c + z, 8 * (1 - c) + z) for c in range(2) for z in range(8)]
    hop = [(z, (z + 1) % 8) for z in range(8)] + [(8 + z, 8 + (z - 1) % 8) for z in range(8)]
    other = lax.ppermute(own, axes, swap)
    block = jnp.concatenate([own, other])
    groups = []
    for _ in range(3):
        block = lax.ppermute(block, axes, hop)
        groups.append((block, lax.ppermute(block, axes, swap)))
    last = lax.ppermute(block[:2], axes, hop)
    return [(own, other, last, lax.ppermute(last, axes, swap))] + groups


def add(a, b):
    return (a.astype(F32) + b.astype(F32)).astype(BF16)


def body(
    attn_out, resid, w_o, norm1_gain, router_w, route_slot, slot_expert, keep,
    w_gate, w_up, w_down, norm2_gain,
):
    joined = jnp.stack([w_gate, w_up])
    weights = lax.all_gather(joined, ("core", "blk"), axis=0, tiled=False)
    weights = weights.reshape(2, 8, 2, 2, CHUNK, FF)
    weights = pltpu.with_memory_space_constraint(weights, pltpu.HBM)
    downs = down_groups(w_down)

    slot_row = jnp.full((1, 128), -1, jnp.int32).at[0, :SLOTS].set(slot_expert)
    hidden, normed, weight = entry(
        attn_out, resid, w_o, norm1_gain.reshape(1, D), router_w, route_slot, slot_row,
        keep.reshape(ROWS, 1),
    )
    place = jnp.stack([lax.axis_index(name) for name in ("x", "y", "core", "blk")])
    place = place.astype(jnp.int32)
    slot_weights = gather_plane(weight.reshape(BLOCKS, LOCAL, ROWS), PLANS[0])
    rows = []
    for group, plan in enumerate(PLANS):
        rows += gather_plane(normed[group], plan)
    packed, spread, scale = compact(place, slot_weights, rows)
    act = hidden_units(packed, weights)

    pairs = []
    for group, (big, small, first, other) in enumerate(PLANS):
        send, kept = spread_rows(place, act, scale, spread, downs[group], group)
        got = lax.ppermute(send, big, links(first))
        send, kept = add(kept[4:], got[4:]), add(kept[:4], got[:4])
        got = lax.ppermute(send, big, links(other))
        send, kept = add(kept[2:], got[2:]), add(kept[:2], got[:2])
        got = lax.ppermute(send, small, links(first))
        send, kept = add(kept[1], got[1]), add(kept[0], got[0])
        got = lax.ppermute(send, small, links(other))
        pairs += [kept, got]
    return closing(place, hidden, norm2_gain.reshape(1, D), pairs)


def solution(mesh):
    fine = Mesh(mesh.devices.reshape(4, 4, 2, 8), ("x", "y", "core", "blk"))
    rows = P(("x", "y", "core", "blk"), None)
    slots = P(("x", "y", "core"), "blk", None)
    placed = (
        rows, rows, P(), P(), P(), rows, P(), P(("x", "y", "core", "blk")),
        slots, slots, slots, P(),
    )
    return jax.shard_map(body, mesh=fine, in_specs=placed, out_specs=rows, check_vma=False)
```

```python
import functools

import jax
import jax.numpy as jnp
from jax import lax
from jax.experimental import pallas as pl
from jax.experimental.pallas import tpu as pltpu
from jax.sharding import Mesh
from jax.sharding import PartitionSpec as P

EPS = 1e-05
D = 1536
FF = 512
TOP = 8
SLOTS = 64
ROWS = 128
CAP = 32
BLOCKS = 16
LOCAL = 4
CHUNK = D // 8
GROUP = 2 * CHUNK
F32 = jnp.float32
BF16 = jnp.bfloat16
MIB = 1024 * 1024


def params(mib, *semantics):
    return pltpu.CompilerParams(
        dimension_semantics=semantics or None, vmem_limit_bytes=mib * MIB
    )


PLANS = (("x", "y", 1, 3), ("x", "y", 3, 1), ("y", "x", 1, 3), ("y", "x", 3, 1))


def block_at(plan, x, y, j):
    big, small, first, other = plan
    bit = lambda n: (j >> n) & 1
    low = bit(0) * other ^ bit(1) * first
    high = bit(2) * other ^ bit(3) * first
    if big == "x":
        return 4 * (x ^ high) + (y ^ low)
    return 4 * (x ^ low) + (y ^ high)


def each(count, unroll, step):
    def run(i, carry):
        step(i)
        return carry

    lax.fori_loop(0, count, run, 0, unroll=unroll)


def links(turn):
    return [(i, i ^ turn) for i in range(4)]


def entry_kernel(
    attn_ref, resid_ref, wo_ref, gain_ref, router_ref, route_ref, expert_ref, keep_ref,
    hidden_ref, rows_ref,
):
    step = pl.program_id(0)
    width = wo_ref.shape[1]
    cols = pl.ds(step * width, width)
    hidden_ref[:, cols] = resid_ref[...].astype(F32) + jnp.dot(
        attn_ref[...], wo_ref[...], preferred_element_type=F32
    )

    @pl.when(step == pl.num_programs(0) - 1)
    def _():
        values = hidden_ref[...]
        mean_sq = jnp.mean(values * values, axis=-1, keepdims=True)
        normed = (values * lax.rsqrt(mean_sq + EPS) * gain_ref[...]).astype(BF16)
        logits = lax.dot_general(
            router_ref[...], normed.astype(F32), (((1,), (1,)), ((), ())),
            precision=lax.Precision.HIGHEST, preferred_element_type=F32,
        )
        experts = logits.shape[0]
        pick = lax.broadcasted_iota(jnp.int32, (experts, SLOTS), 0) == expert_ref[...]
        by_slot = lax.dot_general(
            pick.astype(F32), logits, (((0,), (0,)), ((), ())),
            precision=lax.Precision.HIGHEST, preferred_element_type=F32,
        )
        slot = lax.broadcasted_iota(jnp.int32, (SLOTS, ROWS), 0)
        named = slot == route_ref[0:1]
        for k in range(1, TOP):
            named = named | (slot == route_ref[k : k + 1])
        top = jnp.max(jnp.where(named, by_slot, -jnp.inf), axis=0, keepdims=True)
        grown = jnp.where(named, jnp.exp(jnp.where(named, by_slot - top, 0.0)), 0.0)
        probs = grown / jnp.sum(grown, axis=0, keepdims=True)
        live = jnp.where(keep_ref[...] > 0, probs, 0.0).reshape(BLOCKS, LOCAL, ROWS)
        for group in range(LOCAL):
            rows_ref[group, :ROWS] = normed[:, group * GROUP : (group + 1) * GROUP]
            rest = live[:, group]
            for n in range(3):
                part = rest.astype(BF16)
                rows_ref[group, ROWS:, n * ROWS : (n + 1) * ROWS] = part
                rest = rest - part.astype(F32)


def entry(attn_out, resid, w_o, gain, router_w, route_slot, slot_expert, keep):
    steps = 6
    width = D // steps
    whole = lambda shape: pl.BlockSpec(shape, lambda i: (0,) * len(shape))
    return pl.pallas_call(
        entry_kernel,
        grid=(steps,),
        in_specs=[
            whole((ROWS, D)),
            pl.BlockSpec((ROWS, width), lambda i: (0, i)),
            pl.BlockSpec((D, width), lambda i: (0, i)),
            whole(gain.shape),
            whole(router_w.shape),
            whole(route_slot.shape),
            whole(slot_expert.shape),
            whole(keep.shape),
        ],
        out_specs=[whole((ROWS, D)), whole((LOCAL, ROWS + BLOCKS, GROUP))],
        out_shape=[
            jax.ShapeDtypeStruct((ROWS, D), F32),
            jax.ShapeDtypeStruct((LOCAL, ROWS + BLOCKS, GROUP), BF16),
        ],
        compiler_params=params(16, "arbitrary"),
        name="entry",
    )(attn_out, resid, w_o, gain, router_w, route_slot, slot_expert, keep)


def compact_kernel(place_ref, *refs):
    row_refs = refs[:8]
    packed_ref, spread_ref, scale_ref, pick_ref, weight_ref = refs[8:]
    x, y = place_ref[0], place_ref[1]
    half = BLOCKS // 2
    earlier = (
        lax.broadcasted_iota(jnp.int32, (ROWS, ROWS), 0)
        < lax.broadcasted_iota(jnp.int32, (ROWS, ROWS), 1)
    ).astype(BF16)
    rank = lax.broadcasted_iota(jnp.int32, (CAP, ROWS), 0).astype(F32)
    mine = lax.broadcasted_iota(jnp.int32, (BLOCKS, GROUP), 0) == 4 * x + y

    def fetch(ref, group, start, i):
        b = block_at(PLANS[group], x, y, start + i)
        parts = jnp.where(mine, ref[i, ROWS:].astype(F32), 0.0)
        parts = jnp.sum(parts, axis=0, keepdims=True)
        weight_ref[b, group : group + 1] = (
            parts[:, :ROWS] + parts[:, ROWS : 2 * ROWS] + parts[:, 2 * ROWS :]
        )

    def choose(b):
        weight = weight_ref[b]
        hit = weight > 0.0
        place = jnp.dot(hit.astype(BF16), earlier, preferred_element_type=F32)
        place = jnp.where(hit, place, -1.0)
        picks = [rank == place[s : s + 1] for s in range(LOCAL)]
        for s in range(LOCAL):
            scale_ref[s, b] = jnp.sum(
                jnp.where(picks[s], weight[s : s + 1], 0.0), axis=1, keepdims=True
            )
        pick = jnp.concatenate([p.astype(F32) for p in picks], axis=0)
        spread_ref[b] = jnp.transpose(pick).astype(BF16)
        pick_ref[b] = pick.astype(BF16)

    def pack(ref, group, start, i):
        b = block_at(PLANS[group], x, y, start + i)
        packed = jnp.dot(pick_ref[b], ref[i, :ROWS], preferred_element_type=F32).astype(BF16)
        packed_ref[:, b, :, group * GROUP : (group + 1) * GROUP] = packed.reshape(
            LOCAL, CAP, GROUP
        )

    for n, ref in enumerate(row_refs):
        each(half, 2, functools.partial(fetch, ref, n // 2, n % 2 * half))
    each(BLOCKS, 2, choose)
    for n, ref in enumerate(row_refs):
        each(half, 2, functools.partial(pack, ref, n // 2, n % 2 * half))


def compact(place, rows):
    vmem = pl.BlockSpec(memory_space=pltpu.VMEM)
    return pl.pallas_call(
        compact_kernel,
        in_specs=[pl.BlockSpec(memory_space=pltpu.SMEM)] + [vmem] * len(rows),
        out_specs=[vmem] * 3,
        out_shape=[
            jax.ShapeDtypeStruct((LOCAL, BLOCKS, CAP, D), BF16),
            jax.ShapeDtypeStruct((BLOCKS, ROWS, LOCAL * CAP), BF16),
            jax.ShapeDtypeStruct((LOCAL, BLOCKS, CAP, 1), F32),
        ],
        scratch_shapes=[
            pltpu.VMEM((BLOCKS, LOCAL * CAP, ROWS), BF16),
            pltpu.VMEM((BLOCKS, LOCAL, ROWS), F32),
        ],
        compiler_params=params(24),
        name="compact",
    )(place, *rows)


def hidden_units_kernel(packed_ref, gate_ref, up_ref, act_ref):
    rows = packed_ref[0].reshape(BLOCKS * CAP, D)
    width = 256

    def run(i):
        cols = pl.ds(pl.multiple_of(i * width, width), width)
        w_gate = gate_ref[0, :, 0, 0, :, cols].reshape(D, width)
        w_up = up_ref[0, :, 0, 0, :, cols].reshape(D, width)
        gate = jnp.dot(rows, w_gate, preferred_element_type=F32)
        up = jnp.dot(rows, w_up, preferred_element_type=F32)
        act_ref[0, :, cols] = (gate / (1.0 + jnp.exp(-gate)) * up).astype(BF16)

    each(FF // width, 1, run)


def hidden_units(packed, weights):
    def block(which):
        return pl.BlockSpec((1, 8, 1, 1, CHUNK, FF), lambda s: (s // 2, 0, which, s % 2, 0, 0))

    return pl.pallas_call(
        hidden_units_kernel,
        grid=(LOCAL,),
        in_specs=[pl.BlockSpec((1, BLOCKS, CAP, D), lambda s: (s, 0, 0, 0)), block(0), block(1)],
        out_specs=pl.BlockSpec((1, BLOCKS * CAP, FF), lambda s: (s, 0, 0)),
        out_shape=jax.ShapeDtypeStruct((LOCAL, BLOCKS * CAP, FF), BF16),
        compiler_params=params(24, "arbitrary"),
        name="hidden_units",
    )(packed, weights, weights)


def spread_kernel(plan, place_ref, act_ref, scale_ref, spread_ref, *refs):
    down_refs, (send_ref, keep_ref, part_ref) = refs[:-3], refs[-3:]
    x, y, core = place_ref[0], place_ref[1], place_ref[2]
    half = BLOCKS // 2
    for flip in range(2):
        for q in range(2):
            if len(down_refs) == 4:
                pieces = [down_refs[flip][q], down_refs[2 + flip][q]]
            else:
                pieces = [down_refs[0][2 * flip + q], down_refs[1][2 * (1 - flip) + q]]
            slot = 2 * (core ^ flip) + q
            part = lax.dot_general(
                act_ref[slot], jnp.concatenate(pieces), (((1,), (1,)), ((), ())),
                preferred_element_type=F32,
            )
            scale = scale_ref[slot].reshape(BLOCKS * CAP, 1)
            part_ref[:, slot] = (part * scale).astype(BF16).reshape(BLOCKS, CAP, GROUP)

    def back(out_ref, start, i):
        b = block_at(plan, x, y, start + i)
        rows = part_ref[b].reshape(LOCAL * CAP, GROUP)
        out_ref[i] = jnp.dot(spread_ref[b], rows, preferred_element_type=F32).astype(BF16)

    each(half, 2, functools.partial(back, keep_ref, 0))
    each(half, 2, functools.partial(back, send_ref, half))


def spread_rows(place, act, scale, spread, down, group):
    half = BLOCKS // 2
    vmem = pl.BlockSpec(memory_space=pltpu.VMEM)
    return pl.pallas_call(
        functools.partial(spread_kernel, PLANS[group]),
        in_specs=[pl.BlockSpec(memory_space=pltpu.SMEM)] + [vmem] * (3 + len(down)),
        out_specs=[vmem, vmem],
        scratch_shapes=[pltpu.VMEM((BLOCKS, LOCAL, CAP, GROUP), BF16)],
        out_shape=[jax.ShapeDtypeStruct((half, ROWS, GROUP), BF16)] * 2,
        compiler_params=params(16),
        name="spread",
    )(place, act, scale, spread, *down)


def closing_kernel(place_ref, hidden_ref, gain_ref, *refs):
    parts, (out_ref, moe_ref) = refs[:-2], refs[-2:]
    core, z = place_ref[2], place_ref[3]
    step = 1 - 2 * core
    each_group = len(parts) // LOCAL
    for g in range(LOCAL):
        total = sum(ref[...].astype(F32) for ref in parts[g * each_group : (g + 1) * each_group])
        ends = (z, z + 4) if g == 0 else (z - g * step, z + g * step)
        for n, end in enumerate(ends):
            moe_ref[end & 7] = total[:, n * CHUNK : (n + 1) * CHUNK]
    moe = jnp.concatenate([moe_ref[i] for i in range(8)], axis=1)
    mixed = hidden_ref[...] + moe
    mean_sq = jnp.mean(mixed * mixed, axis=-1, keepdims=True)
    out_ref[...] = (mixed * lax.rsqrt(mean_sq + EPS) * gain_ref[...]).astype(BF16)


def closing(place, hidden, gain, parts):
    vmem = pl.BlockSpec(memory_space=pltpu.VMEM)
    return pl.pallas_call(
        closing_kernel,
        in_specs=[pl.BlockSpec(memory_space=pltpu.SMEM)] + [vmem] * (2 + len(parts)),
        out_specs=vmem,
        out_shape=jax.ShapeDtypeStruct((ROWS, D), BF16),
        scratch_shapes=[pltpu.VMEM((8, ROWS, CHUNK), F32)],
        compiler_params=params(8),
        name="closing",
    )(place, hidden, gain, *parts)


def behind(value, *earlier):
    return lax.optimization_barrier((value, *earlier))[0]


def spread_out(rows, own):
    axes = ("core", "blk")
    swap = [(8 * c + z, 8 * (1 - c) + z) for c in range(2) for z in range(8)]
    hop = [(z, (z + 1) % 8) for z in range(8)] + [(8 + z, 8 + (z - 1) % 8) for z in range(8)]
    held = [rows[group][None] for group in range(LOCAL)]
    block, blocks = None, []
    for step in range(4):
        got = []
        for group, (big, small, first, other) in enumerate(PLANS):
            axis = small if step < 2 else big
            turn = first if step % 2 else other
            got.append(lax.ppermute(held[group], axis, links(turn)))
        if step == 0:
            twin = lax.ppermute(behind(own, rows), axes, swap)
            block = jnp.concatenate([own, twin])
        if step < 3:
            held = [jnp.concatenate(both) for both in zip(held, got)]
            block = lax.ppermute(behind(block, *held), axes, hop)
            blocks.append(block)
    last = lax.ppermute(behind(block[:2], *got), axes, hop)
    *pairs, twin_last = [
        lax.ppermute(behind(block, *got), axes, swap) for block in (*blocks, last)
    ]
    downs = [(own, twin, last, twin_last), *zip(blocks, pairs)]
    return [half for both in zip(held, got) for half in both], downs


def add(a, b):
    return (a.astype(F32) + b.astype(F32)).astype(BF16)


def body(
    attn_out, resid, w_o, norm1_gain, router_w, route_slot, slot_expert, keep,
    w_gate, w_up, w_down, norm2_gain,
):
    joined = jnp.stack([w_gate, w_up])
    weights = lax.all_gather(joined, ("core", "blk"), axis=0, tiled=False)
    weights = weights.reshape(2, 8, 2, 2, CHUNK, FF)
    weights = pltpu.with_memory_space_constraint(weights, pltpu.HBM)

    hidden, outgoing = entry(
        attn_out, resid, w_o, norm1_gain.reshape(1, D), router_w.T, route_slot.T,
        slot_expert.reshape(1, SLOTS), keep.reshape(1, ROWS),
    )
    place = jnp.stack([lax.axis_index(name) for name in ("x", "y", "core", "blk")])
    place = place.astype(jnp.int32)
    rows, downs = spread_out(outgoing, w_down)
    packed, spread, scale = compact(place, rows)
    act = hidden_units(packed, weights)

    parts = []
    for group, (big, small, first, other) in enumerate(PLANS):
        send, kept = spread_rows(place, act, scale, spread, downs[group], group)
        got = lax.ppermute(send, big, links(first))
        send, kept = add(kept[4:], got[4:]), add(kept[:4], got[:4])
        got = lax.ppermute(send, big, links(other))
        sums = [add(kept[i], got[i]) for i in range(4)]
        turns = (other, first, first ^ other)
        parts += [sums[0]] + [
            lax.ppermute(sums[i + 1], small, links(turn)) for i, turn in enumerate(turns)
        ]
    return closing(place, hidden, norm2_gain.reshape(1, D), parts)


def solution(mesh):
    fine = Mesh(mesh.devices.reshape(4, 4, 2, 8), ("x", "y", "core", "blk"))
    rows = P(("x", "y", "core", "blk"), None)
    slots = P(("x", "y", "core"), "blk", None)
    placed = (
        rows, rows, P(), P(), P(), rows, P(), P(("x", "y", "core", "blk")),
        slots, slots, slots, P(),
    )
    return jax.shard_map(body, mesh=fine, in_specs=placed, out_specs=rows, check_vma=False)
```

```python
import functools

import jax
import jax.numpy as jnp
from jax import lax
from jax.experimental import pallas as pl
from jax.experimental.pallas import tpu as pltpu
from jax.sharding import Mesh
from jax.sharding import PartitionSpec as P

EPS = 1e-05
D = 1536
FF = 512
TOP = 8
SLOTS = 64
ROWS = 128
CAP = 32
BLOCKS = 16
LOCAL = 4
CHUNK = D // 8
GROUP = 2 * CHUNK
F32 = jnp.float32
BF16 = jnp.bfloat16
MIB = 1024 * 1024


def params(mib, *semantics):
    return pltpu.CompilerParams(
        dimension_semantics=semantics or None, vmem_limit_bytes=mib * MIB
    )


PLANS = (("x", "y", 1, 3), ("x", "y", 3, 1), ("y", "x", 1, 3), ("y", "x", 3, 1))


def block_at(plan, x, y, j):
    big, small, first, other = plan
    bit = lambda n: (j >> n) & 1
    low = bit(0) * other ^ bit(1) * first
    high = bit(2) * other ^ bit(3) * first
    if big == "x":
        return 4 * (x ^ high) + (y ^ low)
    return 4 * (x ^ low) + (y ^ high)


def each(count, unroll, step):
    def run(i, carry):
        step(i)
        return carry

    lax.fori_loop(0, count, run, 0, unroll=unroll)


def links(turn):
    return [(i, i ^ turn) for i in range(4)]


def entry_kernel(
    attn_ref, resid_ref, wo_ref, gain_ref, router_ref, route_ref, expert_ref, keep_ref,
    hidden_ref, rows_ref,
):
    step = pl.program_id(0)
    width = wo_ref.shape[1]
    cols = pl.ds(step * width, width)
    hidden_ref[:, cols] = resid_ref[...].astype(F32) + jnp.dot(
        attn_ref[...], wo_ref[...], preferred_element_type=F32
    )

    @pl.when(step == pl.num_programs(0) - 1)
    def _():
        values = hidden_ref[...]
        mean_sq = jnp.mean(values * values, axis=-1, keepdims=True)
        normed = (values * lax.rsqrt(mean_sq + EPS) * gain_ref[...]).astype(BF16)
        logits = lax.dot_general(
            router_ref[...], normed.astype(F32), (((1,), (1,)), ((), ())),
            precision=lax.Precision.HIGHEST, preferred_element_type=F32,
        )
        experts = logits.shape[0]
        pick = lax.broadcasted_iota(jnp.int32, (experts, SLOTS), 0) == expert_ref[...]
        by_slot = lax.dot_general(
            pick.astype(F32), logits, (((0,), (0,)), ((), ())),
            precision=lax.Precision.HIGHEST, preferred_element_type=F32,
        )
        slot = lax.broadcasted_iota(jnp.int32, (SLOTS, ROWS), 0)
        named = slot == route_ref[0:1]
        for k in range(1, TOP):
            named = named | (slot == route_ref[k : k + 1])
        top = jnp.max(jnp.where(named, by_slot, -jnp.inf), axis=0, keepdims=True)
        grown = jnp.where(named, jnp.exp(jnp.where(named, by_slot - top, 0.0)), 0.0)
        probs = grown / jnp.sum(grown, axis=0, keepdims=True)
        live = jnp.where(keep_ref[...] > 0, probs, 0.0).reshape(BLOCKS, LOCAL, ROWS)
        for group in range(LOCAL):
            rows_ref[group, :ROWS] = normed[:, group * GROUP : (group + 1) * GROUP]
            rest = live[:, group]
            for n in range(3):
                part = rest.astype(BF16)
                rows_ref[group, ROWS:, n * ROWS : (n + 1) * ROWS] = part
                rest = rest - part.astype(F32)


def entry(attn_out, resid, w_o, gain, router_w, route_slot, slot_expert, keep):
    steps = 6
    width = D // steps
    whole = lambda shape: pl.BlockSpec(shape, lambda i: (0,) * len(shape))
    return pl.pallas_call(
        entry_kernel,
        grid=(steps,),
        in_specs=[
            whole((ROWS, D)),
            pl.BlockSpec((ROWS, width), lambda i: (0, i)),
            pl.BlockSpec((D, width), lambda i: (0, i)),
            whole(gain.shape),
            whole(router_w.shape),
            whole(route_slot.shape),
            whole(slot_expert.shape),
            whole(keep.shape),
        ],
        out_specs=[whole((ROWS, D)), whole((LOCAL, ROWS + BLOCKS, GROUP))],
        out_shape=[
            jax.ShapeDtypeStruct((ROWS, D), F32),
            jax.ShapeDtypeStruct((LOCAL, ROWS + BLOCKS, GROUP), BF16),
        ],
        compiler_params=params(16, "arbitrary"),
        name="entry",
    )(attn_out, resid, w_o, gain, router_w, route_slot, slot_expert, keep)


def compact_kernel(place_ref, *refs):
    row_refs = refs[:8]
    packed_ref, spread_ref, scale_ref, pick_ref, weight_ref = refs[8:]
    x, y = place_ref[0], place_ref[1]
    half = BLOCKS // 2
    earlier = (
        lax.broadcasted_iota(jnp.int32, (ROWS, ROWS), 0)
        < lax.broadcasted_iota(jnp.int32, (ROWS, ROWS), 1)
    ).astype(BF16)
    rank = lax.broadcasted_iota(jnp.int32, (CAP, ROWS), 0).astype(F32)
    mine = lax.broadcasted_iota(jnp.int32, (BLOCKS, GROUP), 0) == 4 * x + y

    def fetch(ref, group, start, i):
        b = block_at(PLANS[group], x, y, start + i)
        parts = jnp.where(mine, ref[i, ROWS:].astype(F32), 0.0)
        parts = jnp.sum(parts, axis=0, keepdims=True)
        weight_ref[b, group : group + 1] = (
            parts[:, :ROWS] + parts[:, ROWS : 2 * ROWS] + parts[:, 2 * ROWS :]
        )

    def choose(b):
        weight = weight_ref[b]
        hit = weight > 0.0
        place = jnp.dot(hit.astype(BF16), earlier, preferred_element_type=F32)
        place = jnp.where(hit, place, -1.0)
        picks = [rank == place[s : s + 1] for s in range(LOCAL)]
        for s in range(LOCAL):
            scale_ref[s, b] = jnp.sum(
                jnp.where(picks[s], weight[s : s + 1], 0.0), axis=1, keepdims=True
            )
        pick = jnp.concatenate([p.astype(F32) for p in picks], axis=0)
        spread_ref[b] = jnp.transpose(pick).astype(BF16)
        pick_ref[b] = pick.astype(BF16)

    def pack(ref, group, start, i):
        b = block_at(PLANS[group], x, y, start + i)
        packed = jnp.dot(pick_ref[b], ref[i, :ROWS], preferred_element_type=F32).astype(BF16)
        packed_ref[:, b, :, group * GROUP : (group + 1) * GROUP] = packed.reshape(
            LOCAL, CAP, GROUP
        )

    for n, ref in enumerate(row_refs):
        each(half, 2, functools.partial(fetch, ref, n // 2, n % 2 * half))
    each(BLOCKS, 2, choose)
    for n, ref in enumerate(row_refs):
        each(half, 2, functools.partial(pack, ref, n // 2, n % 2 * half))


def compact(place, rows):
    vmem = pl.BlockSpec(memory_space=pltpu.VMEM)
    return pl.pallas_call(
        compact_kernel,
        in_specs=[pl.BlockSpec(memory_space=pltpu.SMEM)] + [vmem] * len(rows),
        out_specs=[vmem] * 3,
        out_shape=[
            jax.ShapeDtypeStruct((LOCAL, BLOCKS, CAP, D), BF16),
            jax.ShapeDtypeStruct((BLOCKS, ROWS, LOCAL * CAP), BF16),
            jax.ShapeDtypeStruct((LOCAL, BLOCKS, CAP, 1), F32),
        ],
        scratch_shapes=[
            pltpu.VMEM((BLOCKS, LOCAL * CAP, ROWS), BF16),
            pltpu.VMEM((BLOCKS, LOCAL, ROWS), F32),
        ],
        compiler_params=params(24),
        name="compact",
    )(place, *rows)


def hidden_units_kernel(packed_ref, gate_ref, up_ref, act_ref):
    rows = packed_ref[0].reshape(BLOCKS * CAP, D)
    width = act_ref.shape[-1]
    gate = jnp.dot(rows, gate_ref[...].reshape(D, width), preferred_element_type=F32)
    up = jnp.dot(rows, up_ref[...].reshape(D, width), preferred_element_type=F32)
    act = (gate / (1.0 + jnp.exp(-gate)) * up).astype(BF16)
    act_ref[0] = act.reshape(BLOCKS, CAP, width)


def hidden_units(packed, weights):
    width = 256

    def block(which):
        return pl.BlockSpec(
            (1, 8, 1, 1, CHUNK, width), lambda s, f: (s // 2, 0, which, s % 2, 0, f)
        )

    return pl.pallas_call(
        hidden_units_kernel,
        grid=(LOCAL, FF // width),
        in_specs=[pl.BlockSpec((1, BLOCKS, CAP, D), lambda s, f: (s, 0, 0, 0)), block(0), block(1)],
        out_specs=pl.BlockSpec((1, BLOCKS, CAP, width), lambda s, f: (s, 0, 0, f)),
        out_shape=jax.ShapeDtypeStruct((LOCAL, BLOCKS, CAP, FF), BF16),
        compiler_params=params(24, "arbitrary", "arbitrary"),
        name="hidden_units",
    )(packed, weights, weights)


def spread_kernel(plan, start, place_ref, act_ref, down_ref, scale_ref, spread_ref, out_ref, part_ref):
    x, y = place_ref[0], place_ref[1]
    half = BLOCKS // 2
    order = [block_at(plan, x, y, start + i) for i in range(half)]
    for s in range(LOCAL):
        rows = jnp.concatenate([act_ref[s, b] for b in order])
        scale = jnp.concatenate([scale_ref[s, b] for b in order])
        down = down_ref[s // 2, :, 0, s % 2].reshape(GROUP, FF)
        part = lax.dot_general(
            rows, down, (((1,), (1,)), ((), ())), preferred_element_type=F32
        )
        part_ref[:, s] = (part * scale).astype(BF16).reshape(half, CAP, GROUP)

    def back(i):
        b = block_at(plan, x, y, start + i)
        rows = part_ref[i].reshape(LOCAL * CAP, GROUP)
        out_ref[i] = jnp.dot(spread_ref[b], rows, preferred_element_type=F32).astype(BF16)

    each(half, 4, back)


def spread_rows(place, act, weights, scale, spread, group, start):
    half = BLOCKS // 2
    whole = lambda array: pl.BlockSpec(array.shape, lambda i, o: (0,) * array.ndim)
    return pl.pallas_call(
        functools.partial(spread_kernel, PLANS[group], start),
        grid_spec=pltpu.PrefetchScalarGridSpec(
            num_scalar_prefetch=1,
            grid=(1,),
            in_specs=[
                whole(act),
                pl.BlockSpec((2, 2, 1, 2, CHUNK, FF), lambda i, o: (0, group, 2, 0, 0, 0)),
                whole(scale),
                whole(spread),
            ],
            out_specs=pl.BlockSpec((half, ROWS, GROUP), lambda i, o: (0, 0, 0)),
            scratch_shapes=[pltpu.VMEM((half, LOCAL, CAP, GROUP), BF16)],
        ),
        out_shape=jax.ShapeDtypeStruct((half, ROWS, GROUP), BF16),
        compiler_params=params(16, "arbitrary"),
        name="spread",
    )(place, act, weights, scale, spread)


def closing_kernel(hidden_ref, gain_ref, *refs):
    pairs, out_ref = refs[:-1], refs[-1]
    moe = jnp.concatenate(
        [
            pairs[2 * g][...].astype(F32) + pairs[2 * g + 1][...].astype(F32)
            for g in range(LOCAL)
        ],
        axis=1,
    )
    mixed = hidden_ref[...] + moe
    mean_sq = jnp.mean(mixed * mixed, axis=-1, keepdims=True)
    out_ref[...] = (mixed * lax.rsqrt(mean_sq + EPS) * gain_ref[...]).astype(BF16)


def closing(hidden, gain, pairs):
    return pl.pallas_call(
        closing_kernel,
        out_shape=jax.ShapeDtypeStruct((ROWS, D), BF16),
        compiler_params=params(8),
        name="closing",
    )(hidden, gain, *pairs)


def spread_out(rows):
    halves = []
    for group, (big, small, first, other) in enumerate(PLANS):
        held = rows[group][None]
        for axis, turn in ((small, other), (small, first), (big, other)):
            held = jnp.concatenate([held, lax.ppermute(held, axis, links(turn))])
        halves += [held, lax.ppermute(held, big, links(first))]
    return halves


def add(a, b):
    return (a.astype(F32) + b.astype(F32)).astype(BF16)


def body(
    attn_out, resid, w_o, norm1_gain, router_w, route_slot, slot_expert, keep,
    w_gate, w_up, w_down, norm2_gain,
):
    joined = jnp.stack([w_gate, w_up, w_down])
    weights = lax.all_gather(joined, ("core", "blk"), axis=0, tiled=False)
    weights = weights.reshape(2, 8, 3, 2, CHUNK, FF)
    weights = pltpu.with_memory_space_constraint(weights, pltpu.HBM)

    hidden, outgoing = entry(
        attn_out, resid, w_o, norm1_gain.reshape(1, D), router_w.T, route_slot.T,
        slot_expert.reshape(1, SLOTS), keep.reshape(1, ROWS),
    )
    place = jnp.stack([lax.axis_index(name) for name in ("x", "y")]).astype(jnp.int32)
    packed, spread, scale = compact(place, spread_out(outgoing))
    packed = pltpu.with_memory_space_constraint(packed, pltpu.HBM)
    act = hidden_units(packed, weights)

    halves = []
    for start in (BLOCKS // 2, 0):
        done = [half for group in halves for half in group]
        act = lax.optimization_barrier((act, *done))[0]
        halves.append(
            [spread_rows(place, act, weights, scale, spread, g, start) for g in range(LOCAL)]
        )
    pairs = []
    for send, kept, (big, small, first, other) in zip(*halves, PLANS):
        got = lax.ppermute(send, big, links(first))
        send, kept = add(kept[4:], got[4:]), add(kept[:4], got[:4])
        got = lax.ppermute(send, big, links(other))
        send, kept = add(kept[2:], got[2:]), add(kept[:2], got[:2])
        got = lax.ppermute(send, small, links(first))
        send, kept = add(kept[1], got[1]), add(kept[0], got[0])
        pairs += [kept, lax.ppermute(send, small, links(other))]
    return closing(hidden, norm2_gain.reshape(1, D), pairs)


def solution(mesh):
    fine = Mesh(mesh.devices.reshape(4, 4, 2, 8), ("x", "y", "core", "blk"))
    rows = P(("x", "y", "core", "blk"), None)
    slots = P(("x", "y", "core"), "blk", None)
    placed = (
        rows, rows, P(), P(), P(), rows, P(), P(("x", "y", "core", "blk")),
        slots, slots, slots, P(),
    )
    return jax.shard_map(body, mesh=fine, in_specs=placed, out_specs=rows, check_vma=False)
```

```python
import functools

import jax
import jax.numpy as jnp
from jax import lax
from jax.experimental import pallas as pl
from jax.experimental.pallas import tpu as pltpu
from jax.sharding import Mesh
from jax.sharding import PartitionSpec as P

EPS = 1e-05
D = 1536
FF = 512
TOP = 8
SLOTS = 64
ROWS = 128
CAP = 32
BLOCKS = 16
LOCAL = 4
CHUNK = D // 8
GROUP = 2 * CHUNK
F32 = jnp.float32
BF16 = jnp.bfloat16
MIB = 1024 * 1024


def params(mib, *semantics):
    return pltpu.CompilerParams(
        dimension_semantics=semantics or None, vmem_limit_bytes=mib * MIB
    )


PLANS = (("x", "y", 1, 3), ("x", "y", 3, 1), ("y", "x", 1, 3), ("y", "x", 3, 1))


def block_at(plan, x, y, j):
    big, small, first, other = plan
    bit = lambda n: (j >> n) & 1
    low = bit(0) * other ^ bit(1) * first
    high = bit(2) * other ^ bit(3) * first
    if big == "x":
        return 4 * (x ^ high) + (y ^ low)
    return 4 * (x ^ low) + (y ^ high)


def each(count, unroll, step):
    def run(i, carry):
        step(i)
        return carry

    lax.fori_loop(0, count, run, 0, unroll=unroll)


def links(turn):
    return [(i, i ^ turn) for i in range(4)]


def entry_kernel(
    attn_ref, resid_ref, wo_ref, gain_ref, router_ref, route_ref, expert_ref, keep_ref,
    hidden_ref, rows_ref,
):
    step = pl.program_id(0)
    width = wo_ref.shape[1]
    cols = pl.ds(step * width, width)
    hidden_ref[:, cols] = resid_ref[...].astype(F32) + jnp.dot(
        attn_ref[...], wo_ref[...], preferred_element_type=F32
    )

    @pl.when(step == pl.num_programs(0) - 1)
    def _():
        values = hidden_ref[...]
        mean_sq = jnp.mean(values * values, axis=-1, keepdims=True)
        normed = (values * lax.rsqrt(mean_sq + EPS) * gain_ref[...]).astype(BF16)
        logits = lax.dot_general(
            router_ref[...], normed.astype(F32), (((1,), (1,)), ((), ())),
            precision=lax.Precision.HIGHEST, preferred_element_type=F32,
        )
        experts = logits.shape[0]
        pick = lax.broadcasted_iota(jnp.int32, (experts, SLOTS), 0) == expert_ref[...]
        by_slot = lax.dot_general(
            pick.astype(F32), logits, (((0,), (0,)), ((), ())),
            precision=lax.Precision.HIGHEST, preferred_element_type=F32,
        )
        slot = lax.broadcasted_iota(jnp.int32, (SLOTS, ROWS), 0)
        named = slot == route_ref[0:1]
        for k in range(1, TOP):
            named = named | (slot == route_ref[k : k + 1])
        top = jnp.max(jnp.where(named, by_slot, -jnp.inf), axis=0, keepdims=True)
        grown = jnp.where(named, jnp.exp(jnp.where(named, by_slot - top, 0.0)), 0.0)
        probs = grown / jnp.sum(grown, axis=0, keepdims=True)
        live = jnp.where(keep_ref[...] > 0, probs, 0.0).reshape(BLOCKS, LOCAL, ROWS)
        for group in range(LOCAL):
            rows_ref[group, :ROWS] = normed[:, group * GROUP : (group + 1) * GROUP]
            rest = live[:, group]
            for n in range(3):
                part = rest.astype(BF16)
                rows_ref[group, ROWS:, n * ROWS : (n + 1) * ROWS] = part
                rest = rest - part.astype(F32)


def entry(attn_out, resid, w_o, gain, router_w, route_slot, slot_expert, keep):
    steps = 6
    width = D // steps
    whole = lambda shape: pl.BlockSpec(shape, lambda i: (0,) * len(shape))
    return pl.pallas_call(
        entry_kernel,
        grid=(steps,),
        in_specs=[
            whole((ROWS, D)),
            pl.BlockSpec((ROWS, width), lambda i: (0, i)),
            pl.BlockSpec((D, width), lambda i: (0, i)),
            whole(gain.shape),
            whole(router_w.shape),
            whole(route_slot.shape),
            whole(slot_expert.shape),
            whole(keep.shape),
        ],
        out_specs=[whole((ROWS, D)), whole((LOCAL, ROWS + BLOCKS, GROUP))],
        out_shape=[
            jax.ShapeDtypeStruct((ROWS, D), F32),
            jax.ShapeDtypeStruct((LOCAL, ROWS + BLOCKS, GROUP), BF16),
        ],
        compiler_params=params(16, "arbitrary"),
        name="entry",
    )(attn_out, resid, w_o, gain, router_w, route_slot, slot_expert, keep)


def compact_kernel(place_ref, *refs):
    row_refs = refs[:8]
    packed_ref, spread_ref, scale_ref, pick_ref, weight_ref = refs[8:]
    x, y = place_ref[0], place_ref[1]
    half = BLOCKS // 2
    earlier = (
        lax.broadcasted_iota(jnp.int32, (ROWS, ROWS), 0)
        < lax.broadcasted_iota(jnp.int32, (ROWS, ROWS), 1)
    ).astype(BF16)
    rank = lax.broadcasted_iota(jnp.int32, (CAP, ROWS), 0).astype(F32)
    mine = lax.broadcasted_iota(jnp.int32, (BLOCKS, GROUP), 0) == 4 * x + y

    def fetch(ref, group, start, i):
        b = block_at(PLANS[group], x, y, start + i)
        parts = jnp.where(mine, ref[i, ROWS:].astype(F32), 0.0)
        parts = jnp.sum(parts, axis=0, keepdims=True)
        weight_ref[b, group : group + 1] = (
            parts[:, :ROWS] + parts[:, ROWS : 2 * ROWS] + parts[:, 2 * ROWS :]
        )

    def choose(b):
        weight = weight_ref[b]
        hit = weight > 0.0
        place = jnp.dot(hit.astype(BF16), earlier, preferred_element_type=F32)
        place = jnp.where(hit, place, -1.0)
        picks = [rank == place[s : s + 1] for s in range(LOCAL)]
        for s in range(LOCAL):
            scale_ref[s, b] = jnp.sum(
                jnp.where(picks[s], weight[s : s + 1], 0.0), axis=1, keepdims=True
            )
        pick = jnp.concatenate([p.astype(F32) for p in picks], axis=0)
        spread_ref[b] = jnp.transpose(pick).astype(BF16)
        pick_ref[b] = pick.astype(BF16)

    def pack(ref, group, start, i):
        b = block_at(PLANS[group], x, y, start + i)
        packed = jnp.dot(pick_ref[b], ref[i, :ROWS], preferred_element_type=F32).astype(BF16)
        packed_ref[:, b, :, group * GROUP : (group + 1) * GROUP] = packed.reshape(
            LOCAL, CAP, GROUP
        )

    for n, ref in enumerate(row_refs):
        each(half, 2, functools.partial(fetch, ref, n // 2, n % 2 * half))
    each(BLOCKS, 2, choose)
    for n, ref in enumerate(row_refs):
        each(half, 2, functools.partial(pack, ref, n // 2, n % 2 * half))


def compact(place, rows):
    vmem = pl.BlockSpec(memory_space=pltpu.VMEM)
    return pl.pallas_call(
        compact_kernel,
        in_specs=[pl.BlockSpec(memory_space=pltpu.SMEM)] + [vmem] * len(rows),
        out_specs=[vmem] * 3,
        out_shape=[
            jax.ShapeDtypeStruct((LOCAL, BLOCKS, CAP, D), BF16),
            jax.ShapeDtypeStruct((BLOCKS, ROWS, LOCAL * CAP), BF16),
            jax.ShapeDtypeStruct((LOCAL, BLOCKS, CAP, 1), F32),
        ],
        scratch_shapes=[
            pltpu.VMEM((BLOCKS, LOCAL * CAP, ROWS), BF16),
            pltpu.VMEM((BLOCKS, LOCAL, ROWS), F32),
        ],
        compiler_params=params(24),
        name="compact",
    )(place, *rows)


def hidden_units_kernel(packed_ref, gate_ref, up_ref, act_ref):
    rows = packed_ref[0].reshape(BLOCKS * CAP, D)
    width = act_ref.shape[-1]
    gate = jnp.dot(rows, gate_ref[...].reshape(D, width), preferred_element_type=F32)
    up = jnp.dot(rows, up_ref[...].reshape(D, width), preferred_element_type=F32)
    act = (gate / (1.0 + jnp.exp(-gate)) * up).astype(BF16)
    act_ref[0] = act.reshape(BLOCKS, CAP, width)


def hidden_units(packed, weights):
    width = FF

    def block(which):
        return pl.BlockSpec(
            (1, 8, 1, 1, CHUNK, width), lambda s, f: (s // 2, 0, which, s % 2, 0, f)
        )

    return pl.pallas_call(
        hidden_units_kernel,
        grid=(LOCAL, FF // width),
        in_specs=[pl.BlockSpec((1, BLOCKS, CAP, D), lambda s, f: (s, 0, 0, 0)), block(0), block(1)],
        out_specs=pl.BlockSpec((1, BLOCKS, CAP, width), lambda s, f: (s, 0, 0, f)),
        out_shape=jax.ShapeDtypeStruct((LOCAL, BLOCKS, CAP, FF), BF16),
        compiler_params=params(24, "arbitrary", "arbitrary"),
        name="hidden_units",
    )(packed, weights, weights)


def spread_kernel(start, place_ref, act_ref, scale_ref, spread_ref, weights_ref, *refs):
    out_refs, (down_ref, part_ref, sems) = refs[:LOCAL], refs[LOCAL:]
    x, y = place_ref[0], place_ref[1]
    half = BLOCKS // 2
    copies = [
        pltpu.make_async_copy(
            weights_ref.at[:, 2 * group : 2 * group + 2, 2], down_ref.at[group], sems.at[group]
        )
        for group in range(LOCAL)
    ]
    for copy in copies:
        copy.start()
    for group, plan in enumerate(PLANS):
        order = [block_at(plan, x, y, start + i) for i in range(half)]
        copies[group].wait()
        for s in range(LOCAL):
            rows = jnp.concatenate([act_ref[s, b] for b in order])
            scale = jnp.concatenate([scale_ref[s, b] for b in order])
            down = down_ref[group, s // 2, :, s % 2].reshape(GROUP, FF)
            part = lax.dot_general(
                rows, down, (((1,), (1,)), ((), ())), preferred_element_type=F32
            )
            part_ref[:, s] = (part * scale).astype(BF16).reshape(half, CAP, GROUP)

        def back(i):
            b = block_at(plan, x, y, start + i)
            rows = part_ref[i].reshape(LOCAL * CAP, GROUP)
            out = jnp.dot(spread_ref[b], rows, preferred_element_type=F32)
            out_refs[group][i] = out.astype(BF16)

        each(half, 4, back)


def spread_rows(place, act, weights, scale, spread, start):
    half = BLOCKS // 2
    vmem = pl.BlockSpec(memory_space=pltpu.VMEM)
    return pl.pallas_call(
        functools.partial(spread_kernel, start),
        in_specs=[
            pl.BlockSpec(memory_space=pltpu.SMEM), vmem, vmem, vmem,
            pl.BlockSpec(memory_space=pltpu.HBM),
        ],
        out_specs=[vmem] * LOCAL,
        out_shape=[jax.ShapeDtypeStruct((half, ROWS, GROUP), BF16)] * LOCAL,
        scratch_shapes=[
            pltpu.VMEM((LOCAL, 2, 2, 2, CHUNK, FF), BF16),
            pltpu.VMEM((half, LOCAL, CAP, GROUP), BF16),
            pltpu.SemaphoreType.DMA((LOCAL,)),
        ],
        compiler_params=params(24),
        name="spread",
    )(place, act, scale, spread, weights)


def closing_kernel(hidden_ref, gain_ref, *refs):
    pairs, out_ref = refs[:-1], refs[-1]
    moe = jnp.concatenate(
        [
            pairs[2 * g][...].astype(F32) + pairs[2 * g + 1][...].astype(F32)
            for g in range(LOCAL)
        ],
        axis=1,
    )
    mixed = hidden_ref[...] + moe
    mean_sq = jnp.mean(mixed * mixed, axis=-1, keepdims=True)
    out_ref[...] = (mixed * lax.rsqrt(mean_sq + EPS) * gain_ref[...]).astype(BF16)


def closing(hidden, gain, pairs):
    return pl.pallas_call(
        closing_kernel,
        out_shape=jax.ShapeDtypeStruct((ROWS, D), BF16),
        compiler_params=params(8),
        name="closing",
    )(hidden, gain, *pairs)


def spread_out(rows):
    halves = []
    for group, (big, small, first, other) in enumerate(PLANS):
        held = rows[group][None]
        for axis, turn in ((small, other), (small, first), (big, other)):
            held = jnp.concatenate([held, lax.ppermute(held, axis, links(turn))])
        halves += [held, lax.ppermute(held, big, links(first))]
    return halves


def add(a, b):
    return (a.astype(F32) + b.astype(F32)).astype(BF16)


def body(
    attn_out, resid, w_o, norm1_gain, router_w, route_slot, slot_expert, keep,
    w_gate, w_up, w_down, norm2_gain,
):
    joined = jnp.stack([w_gate, w_up, w_down])
    weights = lax.all_gather(joined, ("core", "blk"), axis=0, tiled=False)
    weights = weights.reshape(2, 8, 3, 2, CHUNK, FF)
    weights = pltpu.with_memory_space_constraint(weights, pltpu.HBM)

    hidden, outgoing = entry(
        attn_out, resid, w_o, norm1_gain.reshape(1, D), router_w.T, route_slot.T,
        slot_expert.reshape(1, SLOTS), keep.reshape(1, ROWS),
    )
    place = jnp.stack([lax.axis_index(name) for name in ("x", "y")]).astype(jnp.int32)
    packed, spread, scale = compact(place, spread_out(outgoing))
    packed = pltpu.with_memory_space_constraint(packed, pltpu.HBM)
    act = hidden_units(packed, weights)

    sends = spread_rows(place, act, weights, scale, spread, BLOCKS // 2)
    act = lax.optimization_barrier((act, *sends))[0]
    halves = [sends, spread_rows(place, act, weights, scale, spread, 0)]
    pairs = []
    for send, kept, (big, small, first, other) in zip(*halves, PLANS):
        got = lax.ppermute(send, big, links(first))
        send, kept = add(kept[4:], got[4:]), add(kept[:4], got[:4])
        got = lax.ppermute(send, big, links(other))
        send, kept = add(kept[2:], got[2:]), add(kept[:2], got[:2])
        got = lax.ppermute(send, small, links(first))
        send, kept = add(kept[1], got[1]), add(kept[0], got[0])
        pairs += [kept, lax.ppermute(send, small, links(other))]
    return closing(hidden, norm2_gain.reshape(1, D), pairs)


def solution(mesh):
    fine = Mesh(mesh.devices.reshape(4, 4, 2, 8), ("x", "y", "core", "blk"))
    rows = P(("x", "y", "core", "blk"), None)
    slots = P(("x", "y", "core"), "blk", None)
    placed = (
        rows, rows, P(), P(), P(), rows, P(), P(("x", "y", "core", "blk")),
        slots, slots, slots, P(),
    )
    return jax.shard_map(body, mesh=fine, in_specs=placed, out_specs=rows, check_vma=False)
```

```python
import functools

import jax
import jax.numpy as jnp
from jax import lax
from jax.experimental import pallas as pl
from jax.experimental.pallas import tpu as pltpu
from jax.sharding import Mesh
from jax.sharding import PartitionSpec as P

EPS = 1e-05
D = 1536
FF = 512
TOP = 8
SLOTS = 64
ROWS = 128
CAP = 32
BLOCKS = 16
LOCAL = 4
CHUNK = D // 8
GROUPS = 2
GROUP = D // GROUPS
F32 = jnp.float32
BF16 = jnp.bfloat16
MIB = 1024 * 1024


def params(mib, *semantics):
    return pltpu.CompilerParams(
        dimension_semantics=semantics or None, vmem_limit_bytes=mib * MIB
    )


PLANS = ((1, 3), (3, 1))


def block_at(plan, place, j):
    first, other = plan
    x, y, core = place
    bit = lambda n: (j >> n) & 1
    low = bit(0) * other ^ bit(1) * first
    high = bit(2) * other ^ bit(3) * first
    along_x = jnp.where(core == 0, high, low)
    along_y = jnp.where(core == 0, low, high)
    return 4 * (x ^ along_x) + (y ^ along_y)


def place_of(place_ref):
    return place_ref[0], place_ref[1], place_ref[2]


def turned(rows, turn, large):
    pairs = []
    for x in range(4):
        for y in range(4):
            for core in range(2):
                along_x = large == (core == 0)
                to = (x ^ turn, y) if along_x else (x, y ^ turn)
                pairs.append((8 * x + 2 * y + core, 8 * to[0] + 2 * to[1] + core))
    return lax.ppermute(rows, ("x", "y", "core"), pairs)


def each(count, unroll, step):
    def run(i, carry):
        step(i)
        return carry

    lax.fori_loop(0, count, run, 0, unroll=unroll)


def entry_kernel(
    attn_ref, resid_ref, wo_ref, gain_ref, router_ref, route_ref, expert_ref, keep_ref,
    hidden_ref, rows_ref,
):
    step = pl.program_id(0)
    width = wo_ref.shape[1]
    cols = pl.ds(step * width, width)
    hidden_ref[:, cols] = resid_ref[...].astype(F32) + jnp.dot(
        attn_ref[...], wo_ref[...], preferred_element_type=F32
    )

    @pl.when(step == pl.num_programs(0) - 1)
    def _():
        values = hidden_ref[...]
        mean_sq = jnp.mean(values * values, axis=-1, keepdims=True)
        normed = (values * lax.rsqrt(mean_sq + EPS) * gain_ref[...]).astype(BF16)
        logits = lax.dot_general(
            router_ref[...], normed.astype(F32), (((1,), (1,)), ((), ())),
            precision=lax.Precision.HIGHEST, preferred_element_type=F32,
        )
        experts = logits.shape[0]
        pick = lax.broadcasted_iota(jnp.int32, (experts, SLOTS), 0) == expert_ref[...]
        by_slot = lax.dot_general(
            pick.astype(F32), logits, (((0,), (0,)), ((), ())),
            precision=lax.Precision.HIGHEST, preferred_element_type=F32,
        )
        slot = lax.broadcasted_iota(jnp.int32, (SLOTS, ROWS), 0)
        named = slot == route_ref[0:1]
        for k in range(1, TOP):
            named = named | (slot == route_ref[k : k + 1])
        top = jnp.max(jnp.where(named, by_slot, -jnp.inf), axis=0, keepdims=True)
        grown = jnp.where(named, jnp.exp(jnp.where(named, by_slot - top, 0.0)), 0.0)
        probs = grown / jnp.sum(grown, axis=0, keepdims=True)
        live = jnp.where(keep_ref[...] > 0, probs, 0.0).reshape(BLOCKS, LOCAL, ROWS)
        for group in range(GROUPS):
            rows_ref[group, :ROWS] = normed[:, group * GROUP : (group + 1) * GROUP]
        for s in range(LOCAL):
            rest = live[:, s]
            for n in range(3):
                part = rest.astype(BF16)
                at = (s % 2 * 3 + n) * ROWS
                rows_ref[s // 2, ROWS:, at : at + ROWS] = part
                rest = rest - part.astype(F32)


def entry(attn_out, resid, w_o, gain, router_w, route_slot, slot_expert, keep):
    steps = 6
    width = D // steps
    whole = lambda shape: pl.BlockSpec(shape, lambda i: (0,) * len(shape))
    return pl.pallas_call(
        entry_kernel,
        grid=(steps,),
        in_specs=[
            whole((ROWS, D)),
            pl.BlockSpec((ROWS, width), lambda i: (0, i)),
            pl.BlockSpec((D, width), lambda i: (0, i)),
            whole(gain.shape),
            whole(router_w.shape),
            whole(route_slot.shape),
            whole(slot_expert.shape),
            whole(keep.shape),
        ],
        out_specs=[whole((ROWS, D)), whole((GROUPS, ROWS + BLOCKS, GROUP))],
        out_shape=[
            jax.ShapeDtypeStruct((ROWS, D), F32),
            jax.ShapeDtypeStruct((GROUPS, ROWS + BLOCKS, GROUP), BF16),
        ],
        compiler_params=params(16, "arbitrary"),
        name="entry",
    )(attn_out, resid, w_o, gain, router_w, route_slot, slot_expert, keep)


def compact_kernel(place_ref, *refs):
    row_refs = refs[: 2 * GROUPS]
    packed_ref, spread_ref, scale_ref, pick_ref, weight_ref = refs[2 * GROUPS :]
    place_here = place_of(place_ref)
    half = BLOCKS // 2
    earlier = (
        lax.broadcasted_iota(jnp.int32, (ROWS, ROWS), 0)
        < lax.broadcasted_iota(jnp.int32, (ROWS, ROWS), 1)
    ).astype(BF16)
    rank = lax.broadcasted_iota(jnp.int32, (CAP, ROWS), 0).astype(F32)
    mine = lax.broadcasted_iota(jnp.int32, (BLOCKS, GROUP), 0) == 4 * place_here[0] + place_here[1]

    def fetch(ref, group, start, i):
        b = block_at(PLANS[group], place_here, start + i)
        parts = jnp.where(mine, ref[i, ROWS:].astype(F32), 0.0)
        parts = jnp.sum(parts, axis=0, keepdims=True)
        parts = [parts[:, n * ROWS : (n + 1) * ROWS] for n in range(6)]
        for n in range(2):
            s = 2 * group + n
            weight_ref[b, s : s + 1] = parts[3 * n] + parts[3 * n + 1] + parts[3 * n + 2]

    def choose(b):
        weight = weight_ref[b]
        hit = weight > 0.0
        place = jnp.dot(hit.astype(BF16), earlier, preferred_element_type=F32)
        place = jnp.where(hit, place, -1.0)
        picks = [rank == place[s : s + 1] for s in range(LOCAL)]
        for s in range(LOCAL):
            scale_ref[s, b] = jnp.sum(
                jnp.where(picks[s], weight[s : s + 1], 0.0), axis=1, keepdims=True
            )
        pick = jnp.concatenate([p.astype(F32) for p in picks], axis=0)
        spread_ref[b] = jnp.transpose(pick).astype(BF16)
        pick_ref[b] = pick.astype(BF16)

    def pack(ref, group, start, i):
        b = block_at(PLANS[group], place_here, start + i)
        packed = jnp.dot(pick_ref[b], ref[i, :ROWS], preferred_element_type=F32).astype(BF16)
        packed_ref[:, b, :, group * GROUP : (group + 1) * GROUP] = packed.reshape(
            LOCAL, CAP, GROUP
        )

    for n, ref in enumerate(row_refs):
        each(half, 2, functools.partial(fetch, ref, n // 2, n % 2 * half))
    each(BLOCKS, 2, choose)
    for n, ref in enumerate(row_refs):
        each(half, 2, functools.partial(pack, ref, n // 2, n % 2 * half))


def compact(place, rows):
    vmem = pl.BlockSpec(memory_space=pltpu.VMEM)
    return pl.pallas_call(
        compact_kernel,
        in_specs=[pl.BlockSpec(memory_space=pltpu.SMEM)] + [vmem] * len(rows),
        out_specs=[vmem] * 3,
        out_shape=[
            jax.ShapeDtypeStruct((LOCAL, BLOCKS, CAP, D), BF16),
            jax.ShapeDtypeStruct((BLOCKS, ROWS, LOCAL * CAP), BF16),
            jax.ShapeDtypeStruct((LOCAL, BLOCKS, CAP, 1), F32),
        ],
        scratch_shapes=[
            pltpu.VMEM((BLOCKS, LOCAL * CAP, ROWS), BF16),
            pltpu.VMEM((BLOCKS, LOCAL, ROWS), F32),
        ],
        compiler_params=params(24),
        name="compact",
    )(place, *rows)


def back_to_rows(plan, place, start, group, act_ref, down_ref, spread_ref, part_ref, out_ref):
    half = BLOCKS // 2
    order = [block_at(plan, place, start + i) for i in range(half)]
    for s in range(LOCAL):
        rows = jnp.concatenate([act_ref[s, b] for b in order])
        down = down_ref[group, s // 2, :, s % 2].reshape(GROUP, FF)
        part = lax.dot_general(
            rows, down, (((1,), (1,)), ((), ())), preferred_element_type=F32
        )
        part_ref[:, s] = part.astype(BF16).reshape(half, CAP, GROUP)

    def back(i):
        b = block_at(plan, place, start + i)
        rows = part_ref[i].reshape(LOCAL * CAP, GROUP)
        out_ref[i] = jnp.dot(spread_ref[b], rows, preferred_element_type=F32).astype(BF16)

    each(half, 4, back)


def experts_kernel(place_ref, packed_hbm, scale_hbm, spread_hbm, weights_hbm, *refs):
    out_refs, act_ref = refs[:GROUPS], refs[GROUPS]
    packed_ref, scale_ref, gate_ref, up_ref, down_ref, spread_ref, part_ref = refs[GROUPS + 1 : -3]
    slot_sems, down_sems, once_sems = refs[-3:]
    blks = 8 // GROUPS
    fetch = pltpu.make_async_copy
    by_slot = [
        [
            fetch(packed_hbm.at[s], packed_ref.at[s], slot_sems.at[s, 0]),
            fetch(weights_hbm.at[s // 2, :, 0, s % 2], gate_ref.at[s], slot_sems.at[s, 1]),
            fetch(weights_hbm.at[s // 2, :, 1, s % 2], up_ref.at[s], slot_sems.at[s, 2]),
        ]
        for s in range(LOCAL)
    ]
    by_group = [
        fetch(weights_hbm.at[:, blks * g : blks * (g + 1), 2], down_ref.at[g], down_sems.at[g])
        for g in range(GROUPS)
    ]
    scales = fetch(scale_hbm, scale_ref, once_sems.at[0])
    spreads = fetch(spread_hbm, spread_ref, once_sems.at[1])
    for copy in (*by_slot[0], scales, *by_slot[1], *by_slot[2], *by_slot[3], *by_group, spreads):
        copy.start()
    for s in range(LOCAL):
        by_slot[s][0].wait()
        by_slot[s][1].wait()
        rows = packed_ref[s].reshape(BLOCKS * CAP, D)
        gate = jnp.dot(rows, gate_ref[s].reshape(D, FF), preferred_element_type=F32)
        by_slot[s][2].wait()
        up = jnp.dot(rows, up_ref[s].reshape(D, FF), preferred_element_type=F32)
        if s == 0:
            scales.wait()
        scale = scale_ref[s].reshape(BLOCKS * CAP, 1)
        act = (gate / (1.0 + jnp.exp(-gate)) * up * scale).astype(BF16)
        act_ref[s] = act.reshape(BLOCKS, CAP, FF)
    spreads.wait()
    for g, plan in enumerate(PLANS):
        by_group[g].wait()
        back_to_rows(
            plan, place_of(place_ref), BLOCKS // 2, g, act_ref, down_ref, spread_ref, part_ref, out_refs[g]
        )


def experts(place, packed, scale, spread, weights):
    half = BLOCKS // 2
    vmem, hbm = pl.BlockSpec(memory_space=pltpu.VMEM), pl.BlockSpec(memory_space=pltpu.HBM)
    return pl.pallas_call(
        experts_kernel,
        in_specs=[pl.BlockSpec(memory_space=pltpu.SMEM), hbm, hbm, hbm, hbm],
        out_specs=[vmem] * (GROUPS + 1),
        out_shape=[jax.ShapeDtypeStruct((half, ROWS, GROUP), BF16)] * GROUPS
        + [jax.ShapeDtypeStruct((LOCAL, BLOCKS, CAP, FF), BF16)],
        scratch_shapes=[
            pltpu.VMEM(packed.shape, BF16),
            pltpu.VMEM(scale.shape, F32),
            pltpu.VMEM((LOCAL, 8, CHUNK, FF), BF16),
            pltpu.VMEM((LOCAL, 8, CHUNK, FF), BF16),
            pltpu.VMEM((GROUPS, 2, 8 // GROUPS, 2, CHUNK, FF), BF16),
            pltpu.VMEM(spread.shape, BF16),
            pltpu.VMEM((half, LOCAL, CAP, GROUP), BF16),
            pltpu.SemaphoreType.DMA((LOCAL, 3)),
            pltpu.SemaphoreType.DMA((GROUPS,)),
            pltpu.SemaphoreType.DMA((2,)),
        ],
        compiler_params=params(48),
        name="experts",
    )(place, packed, scale, spread, weights)


def kept_kernel(place_ref, act_ref, spread_hbm, weights_hbm, *refs):
    out_refs, (down_ref, spread_ref, part_ref, sems) = refs[:GROUPS], refs[GROUPS:]
    blks = 8 // GROUPS
    copies = [
        pltpu.make_async_copy(
            weights_hbm.at[:, blks * g : blks * (g + 1), 2], down_ref.at[g], sems.at[g]
        )
        for g in range(GROUPS)
    ]
    spreads = pltpu.make_async_copy(spread_hbm, spread_ref, sems.at[GROUPS])
    for copy in (copies[0], spreads, *copies[1:]):
        copy.start()
    spreads.wait()
    for g, plan in enumerate(PLANS):
        copies[g].wait()
        back_to_rows(
            plan, place_of(place_ref), 0, g, act_ref, down_ref, spread_ref, part_ref, out_refs[g]
        )


def kept(place, act, spread, weights):
    half = BLOCKS // 2
    vmem, hbm = pl.BlockSpec(memory_space=pltpu.VMEM), pl.BlockSpec(memory_space=pltpu.HBM)
    return pl.pallas_call(
        kept_kernel,
        in_specs=[pl.BlockSpec(memory_space=pltpu.SMEM), vmem, hbm, hbm],
        out_specs=[vmem] * GROUPS,
        out_shape=[jax.ShapeDtypeStruct((half, ROWS, GROUP), BF16)] * GROUPS,
        scratch_shapes=[
            pltpu.VMEM((GROUPS, 2, 8 // GROUPS, 2, CHUNK, FF), BF16),
            pltpu.VMEM(spread.shape, BF16),
            pltpu.VMEM((half, LOCAL, CAP, GROUP), BF16),
            pltpu.SemaphoreType.DMA((GROUPS + 1,)),
        ],
        compiler_params=params(24),
        name="kept",
    )(place, act, spread, weights)


def closing_kernel(hidden_ref, gain_ref, *refs):
    pairs, out_ref = refs[:-1], refs[-1]
    moe = jnp.concatenate(
        [
            pairs[2 * g][...].astype(F32) + pairs[2 * g + 1][...].astype(F32)
            for g in range(GROUPS)
        ],
        axis=1,
    )
    mixed = hidden_ref[...] + moe
    mean_sq = jnp.mean(mixed * mixed, axis=-1, keepdims=True)
    out_ref[...] = (mixed * lax.rsqrt(mean_sq + EPS) * gain_ref[...]).astype(BF16)


def closing(hidden, gain, pairs):
    return pl.pallas_call(
        closing_kernel,
        out_shape=jax.ShapeDtypeStruct((ROWS, D), BF16),
        compiler_params=params(8),
        name="closing",
    )(hidden, gain, *pairs)


def spread_out(rows):
    halves = []
    for group, (first, other) in enumerate(PLANS):
        held = rows[group][None]
        for turn, large in ((other, False), (first, False), (other, True)):
            held = jnp.concatenate([held, turned(held, turn, large)])
        halves += [held, turned(held, first, True)]
    return halves


def add(a, b):
    return (a.astype(F32) + b.astype(F32)).astype(BF16)


def body(
    attn_out, resid, w_o, norm1_gain, router_w, route_slot, slot_expert, keep,
    w_gate, w_up, w_down, norm2_gain,
):
    joined = jnp.stack([w_gate, w_up, w_down])
    weights = lax.all_gather(joined, ("core", "blk"), axis=0, tiled=False)
    weights = weights.reshape(2, 8, 3, 2, CHUNK, FF)
    weights = pltpu.with_memory_space_constraint(weights, pltpu.HBM)

    hidden, outgoing = entry(
        attn_out, resid, w_o, norm1_gain.reshape(1, D), router_w.T, route_slot.T,
        slot_expert.reshape(1, SLOTS), keep.reshape(1, ROWS),
    )
    place = jnp.stack([lax.axis_index(name) for name in ("x", "y", "core")])
    place = place.astype(jnp.int32)
    packed, spread, scale = [
        pltpu.with_memory_space_constraint(array, pltpu.HBM)
        for array in compact(place, spread_out(outgoing))
    ]
    *sends, act = experts(place, packed, scale, spread, weights)
    keeps = kept(place, act, spread, weights)
    pairs = []
    for send, keep, (first, other) in zip(sends, keeps, PLANS):
        got = turned(send, first, True)
        send, keep = add(keep[4:], got[4:]), add(keep[:4], got[:4])
        got = turned(send, other, True)
        send, keep = add(keep[2:], got[2:]), add(keep[:2], got[:2])
        got = turned(send, first, False)
        send, keep = add(keep[1], got[1]), add(keep[0], got[0])
        pairs += [keep, turned(send, other, False)]
    return closing(hidden, norm2_gain.reshape(1, D), pairs)


def solution(mesh):
    fine = Mesh(mesh.devices.reshape(4, 4, 2, 8), ("x", "y", "core", "blk"))
    rows = P(("x", "y", "core", "blk"), None)
    slots = P(("x", "y", "core"), "blk", None)
    placed = (
        rows, rows, P(), P(), P(), rows, P(), P(("x", "y", "core", "blk")),
        slots, slots, slots, P(),
    )
    return jax.shard_map(body, mesh=fine, in_specs=placed, out_specs=rows, check_vma=False)
```

```python
import functools

import jax
import jax.numpy as jnp
from jax import lax
from jax.experimental import pallas as pl
from jax.experimental.pallas import tpu as pltpu
from jax.sharding import Mesh
from jax.sharding import PartitionSpec as P

EPS = 1e-05
D = 1536
FF = 512
TOP = 8
SLOTS = 64
ROWS = 128
CAP = 32
BLOCKS = 16
LOCAL = 4
CHUNK = D // 8
GROUPS = 2
GROUP = D // GROUPS
F32 = jnp.float32
BF16 = jnp.bfloat16
MIB = 1024 * 1024


def params(mib, *semantics):
    return pltpu.CompilerParams(
        dimension_semantics=semantics or None, vmem_limit_bytes=mib * MIB
    )


PLANS = ((1, 3), (3, 1))


def block_at(plan, place, j):
    first, other = plan
    x, y, core = place
    bit = lambda n: (j >> n) & 1
    low = bit(0) * other ^ bit(1) * first
    high = bit(2) * other ^ bit(3) * first
    along_x = jnp.where(core == 0, high, low)
    along_y = jnp.where(core == 0, low, high)
    return 4 * (x ^ along_x) + (y ^ along_y)


def place_of(place_ref):
    return place_ref[0], place_ref[1], place_ref[2]


def turned(rows, turn, large):
    pairs = []
    for x in range(4):
        for y in range(4):
            for core in range(2):
                along_x = large == (core == 0)
                to = (x ^ turn, y) if along_x else (x, y ^ turn)
                pairs.append((8 * x + 2 * y + core, 8 * to[0] + 2 * to[1] + core))
    return lax.ppermute(rows, ("x", "y", "core"), pairs)


def each(count, unroll, step):
    def run(i, carry):
        step(i)
        return carry

    lax.fori_loop(0, count, run, 0, unroll=unroll)


def join_kernel(*refs):
    shards, joined, sems = refs[:-2], refs[-2], refs[-1]
    copies = [
        pltpu.make_async_copy(shard, joined.at[n], sems.at[n]) for n, shard in enumerate(shards)
    ]
    for copy in copies:
        copy.start()
    for copy in copies:
        copy.wait()


def join(*shards):
    hbm = pl.BlockSpec(memory_space=pltpu.HBM)
    return pl.pallas_call(
        join_kernel,
        in_specs=[hbm] * len(shards),
        out_specs=hbm,
        out_shape=jax.ShapeDtypeStruct((len(shards), *shards[0].shape), BF16),
        scratch_shapes=[pltpu.SemaphoreType.DMA((len(shards),))],
        name="join",
    )(*shards)


def entry_kernel(
    attn_ref, resid_ref, wo_ref, gain_ref, router_ref, route_ref, expert_ref, keep_ref,
    hidden_ref, rows_ref,
):
    step = pl.program_id(0)
    width = wo_ref.shape[1]
    cols = pl.ds(step * width, width)
    hidden_ref[:, cols] = resid_ref[...].astype(F32) + jnp.dot(
        attn_ref[...], wo_ref[...], preferred_element_type=F32
    )

    @pl.when(step == pl.num_programs(0) - 1)
    def _():
        values = hidden_ref[...]
        mean_sq = jnp.mean(values * values, axis=-1, keepdims=True)
        normed = (values * lax.rsqrt(mean_sq + EPS) * gain_ref[...]).astype(BF16)
        logits = lax.dot_general(
            router_ref[...], normed.astype(F32), (((1,), (1,)), ((), ())),
            precision=lax.Precision.HIGHEST, preferred_element_type=F32,
        )
        experts = logits.shape[0]
        pick = lax.broadcasted_iota(jnp.int32, (experts, SLOTS), 0) == expert_ref[...]
        by_slot = lax.dot_general(
            pick.astype(F32), logits, (((0,), (0,)), ((), ())),
            precision=lax.Precision.HIGHEST, preferred_element_type=F32,
        )
        slot = lax.broadcasted_iota(jnp.int32, (SLOTS, ROWS), 0)
        named = slot == route_ref[0:1]
        for k in range(1, TOP):
            named = named | (slot == route_ref[k : k + 1])
        top = jnp.max(jnp.where(named, by_slot, -jnp.inf), axis=0, keepdims=True)
        grown = jnp.where(named, jnp.exp(jnp.where(named, by_slot - top, 0.0)), 0.0)
        probs = grown / jnp.sum(grown, axis=0, keepdims=True)
        live = jnp.where(keep_ref[...] > 0, probs, 0.0).reshape(BLOCKS, LOCAL, ROWS)
        for group in range(GROUPS):
            rows_ref[group, :ROWS] = normed[:, group * GROUP : (group + 1) * GROUP]
        for s in range(LOCAL):
            rest = live[:, s]
            for n in range(3):
                part = rest.astype(BF16)
                at = (s % 2 * 3 + n) * ROWS
                rows_ref[s // 2, ROWS:, at : at + ROWS] = part
                rest = rest - part.astype(F32)


def entry(attn_out, resid, w_o, gain, router_w, route_slot, slot_expert, keep):
    steps = 6
    width = D // steps
    whole = lambda shape: pl.BlockSpec(shape, lambda i: (0,) * len(shape))
    return pl.pallas_call(
        entry_kernel,
        grid=(steps,),
        in_specs=[
            whole((ROWS, D)),
            pl.BlockSpec((ROWS, width), lambda i: (0, i)),
            pl.BlockSpec((D, width), lambda i: (0, i)),
            whole(gain.shape),
            whole(router_w.shape),
            whole(route_slot.shape),
            whole(slot_expert.shape),
            whole(keep.shape),
        ],
        out_specs=[whole((ROWS, D)), whole((GROUPS, ROWS + BLOCKS, GROUP))],
        out_shape=[
            jax.ShapeDtypeStruct((ROWS, D), F32),
            jax.ShapeDtypeStruct((GROUPS, ROWS + BLOCKS, GROUP), BF16),
        ],
        compiler_params=params(16, "arbitrary"),
        name="entry",
    )(attn_out, resid, w_o, gain, router_w, route_slot, slot_expert, keep)


def compact_kernel(place_ref, *refs):
    row_refs = refs[: 2 * GROUPS]
    packed_ref, spread_ref, scale_ref, pick_ref, weight_ref = refs[2 * GROUPS :]
    place_here = place_of(place_ref)
    half = BLOCKS // 2
    earlier = (
        lax.broadcasted_iota(jnp.int32, (ROWS, ROWS), 0)
        < lax.broadcasted_iota(jnp.int32, (ROWS, ROWS), 1)
    ).astype(BF16)
    rank = lax.broadcasted_iota(jnp.int32, (CAP, ROWS), 0).astype(F32)
    mine = lax.broadcasted_iota(jnp.int32, (BLOCKS, GROUP), 0) == 4 * place_here[0] + place_here[1]

    def fetch(ref, group, start, i):
        b = block_at(PLANS[group], place_here, start + i)
        parts = jnp.where(mine, ref[i, ROWS:].astype(F32), 0.0)
        parts = jnp.sum(parts, axis=0, keepdims=True)
        parts = [parts[:, n * ROWS : (n + 1) * ROWS] for n in range(6)]
        for n in range(2):
            s = 2 * group + n
            weight_ref[b, s : s + 1] = parts[3 * n] + parts[3 * n + 1] + parts[3 * n + 2]

    def choose(b):
        weight = weight_ref[b]
        hit = weight > 0.0
        place = jnp.dot(hit.astype(BF16), earlier, preferred_element_type=F32)
        place = jnp.where(hit, place, -1.0)
        picks = [rank == place[s : s + 1] for s in range(LOCAL)]
        for s in range(LOCAL):
            scale_ref[s, b] = jnp.sum(
                jnp.where(picks[s], weight[s : s + 1], 0.0), axis=1, keepdims=True
            )
        pick = jnp.concatenate([p.astype(F32) for p in picks], axis=0)
        spread_ref[b] = jnp.transpose(pick).astype(BF16)
        pick_ref[b] = pick.astype(BF16)

    def pack(ref, group, start, i):
        b = block_at(PLANS[group], place_here, start + i)
        packed = jnp.dot(pick_ref[b], ref[i, :ROWS], preferred_element_type=F32).astype(BF16)
        packed_ref[:, b, :, group * GROUP : (group + 1) * GROUP] = packed.reshape(
            LOCAL, CAP, GROUP
        )

    for n, ref in enumerate(row_refs):
        each(half, 2, functools.partial(fetch, ref, n // 2, n % 2 * half))
    each(BLOCKS, 2, choose)
    for n, ref in enumerate(row_refs):
        each(half, 2, functools.partial(pack, ref, n // 2, n % 2 * half))


def compact(place, rows):
    vmem = pl.BlockSpec(memory_space=pltpu.VMEM)
    return pl.pallas_call(
        compact_kernel,
        in_specs=[pl.BlockSpec(memory_space=pltpu.SMEM)] + [vmem] * len(rows),
        out_specs=[vmem] * 3,
        out_shape=[
            jax.ShapeDtypeStruct((LOCAL, BLOCKS, CAP, D), BF16),
            jax.ShapeDtypeStruct((BLOCKS, ROWS, LOCAL * CAP), BF16),
            jax.ShapeDtypeStruct((LOCAL, BLOCKS, CAP, 1), F32),
        ],
        scratch_shapes=[
            pltpu.VMEM((BLOCKS, LOCAL * CAP, ROWS), BF16),
            pltpu.VMEM((BLOCKS, LOCAL, ROWS), F32),
        ],
        compiler_params=params(24),
        name="compact",
    )(place, *rows)


def back_to_rows(plan, place, start, group, act_ref, down_ref, spread_ref, part_ref, out_refs):
    half = BLOCKS // 2
    order = [block_at(plan, place, start + i) for i in range(half)]
    for s in range(LOCAL):
        rows = jnp.concatenate([act_ref[s, b] for b in order])
        down = down_ref[group, s // 2, :, s % 2].reshape(GROUP, FF)
        part = lax.dot_general(
            rows, down, (((1,), (1,)), ((), ())), preferred_element_type=F32
        )
        part_ref[:, s] = part.astype(BF16).reshape(half, CAP, GROUP)

    def back(out_ref, first, i):
        b = block_at(plan, place, start + first + i)
        rows = part_ref[first + i].reshape(LOCAL * CAP, GROUP)
        out_ref[i] = jnp.dot(spread_ref[b], rows, preferred_element_type=F32).astype(BF16)

    for n, out_ref in enumerate(out_refs):
        each(half // 2, 4, functools.partial(back, out_ref, n * half // 2))


def experts_kernel(place_ref, packed_hbm, scale_hbm, spread_hbm, weights_hbm, *refs):
    out_refs, act_ref = refs[: 2 * GROUPS], refs[2 * GROUPS]
    packed_ref, scale_ref, gate_ref, up_ref, down_ref, spread_ref, part_ref = refs[2 * GROUPS + 1 : -3]
    slot_sems, down_sems, once_sems = refs[-3:]
    blks = 8 // GROUPS
    fetch = pltpu.make_async_copy
    by_slot = [
        [
            fetch(packed_hbm.at[s], packed_ref.at[s], slot_sems.at[s, 0]),
            fetch(weights_hbm.at[s // 2, :, 0, s % 2], gate_ref.at[s], slot_sems.at[s, 1]),
            fetch(weights_hbm.at[s // 2, :, 1, s % 2], up_ref.at[s], slot_sems.at[s, 2]),
        ]
        for s in range(LOCAL)
    ]
    by_group = [
        fetch(weights_hbm.at[:, blks * g : blks * (g + 1), 2], down_ref.at[g], down_sems.at[g])
        for g in range(GROUPS)
    ]
    scales = fetch(scale_hbm, scale_ref, once_sems.at[0])
    spreads = fetch(spread_hbm, spread_ref, once_sems.at[1])
    for copy in (*by_slot[0], scales, *by_slot[1], *by_slot[2], *by_slot[3], *by_group, spreads):
        copy.start()
    for s in range(LOCAL):
        by_slot[s][0].wait()
        by_slot[s][1].wait()
        rows = packed_ref[s].reshape(BLOCKS * CAP, D)
        gate = jnp.dot(rows, gate_ref[s].reshape(D, FF), preferred_element_type=F32)
        by_slot[s][2].wait()
        up = jnp.dot(rows, up_ref[s].reshape(D, FF), preferred_element_type=F32)
        if s == 0:
            scales.wait()
        scale = scale_ref[s].reshape(BLOCKS * CAP, 1)
        act = (gate / (1.0 + jnp.exp(-gate)) * up * scale).astype(BF16)
        act_ref[s] = act.reshape(BLOCKS, CAP, FF)
    spreads.wait()
    for g, plan in enumerate(PLANS):
        by_group[g].wait()
        back_to_rows(
            plan, place_of(place_ref), BLOCKS // 2, g, act_ref, down_ref, spread_ref, part_ref,
            out_refs[2 * g : 2 * g + 2],
        )


def experts(place, packed, scale, spread, weights):
    half = BLOCKS // 2
    vmem, hbm = pl.BlockSpec(memory_space=pltpu.VMEM), pl.BlockSpec(memory_space=pltpu.HBM)
    return pl.pallas_call(
        experts_kernel,
        in_specs=[pl.BlockSpec(memory_space=pltpu.SMEM), hbm, hbm, hbm, hbm],
        out_specs=[vmem] * (2 * GROUPS + 1),
        out_shape=[jax.ShapeDtypeStruct((half // 2, ROWS, GROUP), BF16)] * (2 * GROUPS)
        + [jax.ShapeDtypeStruct((LOCAL, BLOCKS, CAP, FF), BF16)],
        scratch_shapes=[
            pltpu.VMEM(packed.shape, BF16),
            pltpu.VMEM(scale.shape, F32),
            pltpu.VMEM((LOCAL, 8, CHUNK, FF), BF16),
            pltpu.VMEM((LOCAL, 8, CHUNK, FF), BF16),
            pltpu.VMEM((GROUPS, 2, 8 // GROUPS, 2, CHUNK, FF), BF16),
            pltpu.VMEM(spread.shape, BF16),
            pltpu.VMEM((half, LOCAL, CAP, GROUP), BF16),
            pltpu.SemaphoreType.DMA((LOCAL, 3)),
            pltpu.SemaphoreType.DMA((GROUPS,)),
            pltpu.SemaphoreType.DMA((2,)),
        ],
        compiler_params=params(48),
        name="experts",
    )(place, packed, scale, spread, weights)


def kept_kernel(place_ref, act_ref, spread_hbm, weights_hbm, *refs):
    out_refs, (down_ref, spread_ref, part_ref, sems) = refs[: 2 * GROUPS], refs[2 * GROUPS :]
    blks = 8 // GROUPS
    copies = [
        pltpu.make_async_copy(
            weights_hbm.at[:, blks * g : blks * (g + 1), 2], down_ref.at[g], sems.at[g]
        )
        for g in range(GROUPS)
    ]
    spreads = pltpu.make_async_copy(spread_hbm, spread_ref, sems.at[GROUPS])
    for copy in (copies[0], spreads, *copies[1:]):
        copy.start()
    spreads.wait()
    for g, plan in enumerate(PLANS):
        copies[g].wait()
        back_to_rows(
            plan, place_of(place_ref), 0, g, act_ref, down_ref, spread_ref, part_ref,
            out_refs[2 * g : 2 * g + 2],
        )


def kept(place, act, spread, weights):
    half = BLOCKS // 2
    vmem, hbm = pl.BlockSpec(memory_space=pltpu.VMEM), pl.BlockSpec(memory_space=pltpu.HBM)
    return pl.pallas_call(
        kept_kernel,
        in_specs=[pl.BlockSpec(memory_space=pltpu.SMEM), vmem, hbm, hbm],
        out_specs=[vmem] * (2 * GROUPS),
        out_shape=[jax.ShapeDtypeStruct((half // 2, ROWS, GROUP), BF16)] * (2 * GROUPS),
        scratch_shapes=[
            pltpu.VMEM((GROUPS, 2, 8 // GROUPS, 2, CHUNK, FF), BF16),
            pltpu.VMEM(spread.shape, BF16),
            pltpu.VMEM((half, LOCAL, CAP, GROUP), BF16),
            pltpu.SemaphoreType.DMA((GROUPS + 1,)),
        ],
        compiler_params=params(24),
        name="kept",
    )(place, act, spread, weights)


def closing_kernel(hidden_ref, gain_ref, *refs):
    parts, out_ref = refs[:-1], refs[-1]
    moe = jnp.concatenate(
        [sum(ref[...].astype(F32) for ref in parts[4 * g : 4 * g + 4]) for g in range(GROUPS)],
        axis=1,
    )
    mixed = hidden_ref[...] + moe
    mean_sq = jnp.mean(mixed * mixed, axis=-1, keepdims=True)
    out_ref[...] = (mixed * lax.rsqrt(mean_sq + EPS) * gain_ref[...]).astype(BF16)


def closing(hidden, gain, parts):
    return pl.pallas_call(
        closing_kernel,
        out_shape=jax.ShapeDtypeStruct((ROWS, D), BF16),
        compiler_params=params(8),
        name="closing",
    )(hidden, gain, *parts)


def spread_out(rows):
    halves = []
    for group, (first, other) in enumerate(PLANS):
        held = rows[group][None]
        for turn, large in ((other, False), (first, False), (other, True)):
            held = jnp.concatenate([held, turned(held, turn, large)])
        halves += [held, turned(held, first, True)]
    return halves


def add(a, b):
    return (a.astype(F32) + b.astype(F32)).astype(BF16)


def body(
    attn_out, resid, w_o, norm1_gain, router_w, route_slot, slot_expert, keep,
    w_gate, w_up, w_down, norm2_gain,
):
    joined = join(w_gate, w_up, w_down)
    weights = lax.all_gather(joined, ("core", "blk"), axis=0, tiled=False)
    weights = weights.reshape(2, 8, 3, 2, CHUNK, FF)
    weights = pltpu.with_memory_space_constraint(weights, pltpu.HBM)

    hidden, outgoing = entry(
        attn_out, resid, w_o, norm1_gain.reshape(1, D), router_w.T, route_slot.T,
        slot_expert.reshape(1, SLOTS), keep.reshape(1, ROWS),
    )
    place = jnp.stack([lax.axis_index(name) for name in ("x", "y", "core")])
    place = place.astype(jnp.int32)
    packed, spread, scale = [
        pltpu.with_memory_space_constraint(array, pltpu.HBM)
        for array in compact(place, spread_out(outgoing))
    ]
    *sends, act = experts(place, packed, scale, spread, weights)
    keeps = kept(place, act, spread, weights)
    parts = []
    for group, (first, other) in enumerate(PLANS):
        last, soon = sends[2 * group : 2 * group + 2]
        held, passed = keeps[2 * group : 2 * group + 2]
        passed = add(passed, turned(soon, first, True))
        held = add(held, turned(last, first, True))
        got = turned(passed, other, True)
        sums = [add(held[i], got[i]) for i in range(4)]
        turns = (other, first, first ^ other)
        parts += [sums[0]] + [turned(sums[i + 1], turn, False) for i, turn in enumerate(turns)]
    return closing(hidden, norm2_gain.reshape(1, D), parts)


def solution(mesh):
    fine = Mesh(mesh.devices.reshape(4, 4, 2, 8), ("x", "y", "core", "blk"))
    rows = P(("x", "y", "core", "blk"), None)
    slots = P(("x", "y", "core"), "blk", None)
    placed = (
        rows, rows, P(), P(), P(), rows, P(), P(("x", "y", "core", "blk")),
        slots, slots, slots, P(),
    )
    return jax.shard_map(body, mesh=fine, in_specs=placed, out_specs=rows, check_vma=False)
```

```python
import functools

import jax
import jax.numpy as jnp
from jax import lax
from jax.experimental import pallas as pl
from jax.experimental.pallas import tpu as pltpu
from jax.sharding import Mesh
from jax.sharding import PartitionSpec as P

EPS = 1e-05
D = 1536
FF = 512
TOP = 8
SLOTS = 64
ROWS = 128
CAP = 32
BLOCKS = 16
LOCAL = 4
CHUNK = D // 8
GROUPS = 2
GROUP = D // GROUPS
F32 = jnp.float32
BF16 = jnp.bfloat16
MIB = 1024 * 1024


def params(mib, *semantics):
    return pltpu.CompilerParams(
        dimension_semantics=semantics or None, vmem_limit_bytes=mib * MIB
    )


PLANS = ((1, 3), (3, 1))


def block_at(plan, place, j):
    first, other = plan
    x, y, core = place
    bit = lambda n: (j >> n) & 1
    low = bit(0) * other ^ bit(1) * first
    high = bit(2) * other ^ bit(3) * first
    along_x = jnp.where(core == 0, high, low)
    along_y = jnp.where(core == 0, low, high)
    return 4 * (x ^ along_x) + (y ^ along_y)


def place_of(place_ref):
    return place_ref[0], place_ref[1], place_ref[2]


def turned(rows, turn, large):
    pairs = []
    for x in range(4):
        for y in range(4):
            for core in range(2):
                along_x = large == (core == 0)
                to = (x ^ turn, y) if along_x else (x, y ^ turn)
                pairs.append((8 * x + 2 * y + core, 8 * to[0] + 2 * to[1] + core))
    return lax.ppermute(rows, ("x", "y", "core"), pairs)


def each(count, unroll, step):
    def run(i, carry):
        step(i)
        return carry

    lax.fori_loop(0, count, run, 0, unroll=unroll)


def join_kernel(*refs):
    count = len(refs) - 3
    shards, joined, held, sems = refs[:count], refs[count], refs[count + 1], refs[count + 2]
    inward = [
        pltpu.make_async_copy(shard, held.at[n], sems.at[0, n]) for n, shard in enumerate(shards)
    ]
    outward = [
        pltpu.make_async_copy(held.at[n], joined.at[n], sems.at[1, n]) for n in range(count)
    ]
    for copy in inward:
        copy.start()
    for n in range(count):
        inward[n].wait()
        outward[n].start()
    for copy in outward:
        copy.wait()


def join(*shards):
    hbm = pl.BlockSpec(memory_space=pltpu.HBM)
    shape = (len(shards), *shards[0].shape)
    return pl.pallas_call(
        join_kernel,
        in_specs=[hbm] * len(shards),
        out_specs=hbm,
        out_shape=jax.ShapeDtypeStruct(shape, BF16),
        scratch_shapes=[pltpu.VMEM(shape, BF16), pltpu.SemaphoreType.DMA((2, len(shards)))],
        name="join",
    )(*shards)


def entry_kernel(
    attn_ref, resid_ref, wo_ref, gain_ref, router_ref, route_ref, expert_ref, keep_ref,
    hidden_ref, rows_ref,
):
    step = pl.program_id(0)
    width = wo_ref.shape[1]
    cols = pl.ds(step * width, width)
    hidden_ref[:, cols] = resid_ref[...].astype(F32) + jnp.dot(
        attn_ref[...], wo_ref[...], preferred_element_type=F32
    )

    @pl.when(step == pl.num_programs(0) - 1)
    def _():
        values = hidden_ref[...]
        mean_sq = jnp.mean(values * values, axis=-1, keepdims=True)
        normed = (values * lax.rsqrt(mean_sq + EPS) * gain_ref[...]).astype(BF16)
        logits = lax.dot_general(
            router_ref[...], normed.astype(F32), (((1,), (1,)), ((), ())),
            precision=lax.Precision.HIGHEST, preferred_element_type=F32,
        )
        experts = logits.shape[0]
        pick = lax.broadcasted_iota(jnp.int32, (experts, SLOTS), 0) == expert_ref[...]
        by_slot = lax.dot_general(
            pick.astype(F32), logits, (((0,), (0,)), ((), ())),
            precision=lax.Precision.HIGHEST, preferred_element_type=F32,
        )
        slot = lax.broadcasted_iota(jnp.int32, (SLOTS, ROWS), 0)
        named = slot == route_ref[0:1]
        for k in range(1, TOP):
            named = named | (slot == route_ref[k : k + 1])
        top = jnp.max(jnp.where(named, by_slot, -jnp.inf), axis=0, keepdims=True)
        grown = jnp.where(named, jnp.exp(jnp.where(named, by_slot - top, 0.0)), 0.0)
        probs = grown / jnp.sum(grown, axis=0, keepdims=True)
        live = jnp.where(keep_ref[...] > 0, probs, 0.0).reshape(BLOCKS, LOCAL, ROWS)
        for group in range(GROUPS):
            rows_ref[group, :ROWS] = normed[:, group * GROUP : (group + 1) * GROUP]
        for s in range(LOCAL):
            rest = live[:, s]
            for n in range(3):
                part = rest.astype(BF16)
                at = (s % 2 * 3 + n) * ROWS
                rows_ref[s // 2, ROWS:, at : at + ROWS] = part
                rest = rest - part.astype(F32)


def entry(attn_out, resid, w_o, gain, router_w, route_slot, slot_expert, keep):
    steps = 6
    width = D // steps
    whole = lambda shape: pl.BlockSpec(shape, lambda i: (0,) * len(shape))
    return pl.pallas_call(
        entry_kernel,
        grid=(steps,),
        in_specs=[
            whole((ROWS, D)),
            pl.BlockSpec((ROWS, width), lambda i: (0, i)),
            pl.BlockSpec((D, width), lambda i: (0, i)),
            whole(gain.shape),
            whole(router_w.shape),
            whole(route_slot.shape),
            whole(slot_expert.shape),
            whole(keep.shape),
        ],
        out_specs=[whole((ROWS, D)), whole((GROUPS, ROWS + BLOCKS, GROUP))],
        out_shape=[
            jax.ShapeDtypeStruct((ROWS, D), F32),
            jax.ShapeDtypeStruct((GROUPS, ROWS + BLOCKS, GROUP), BF16),
        ],
        compiler_params=params(16, "arbitrary"),
        name="entry",
    )(attn_out, resid, w_o, gain, router_w, route_slot, slot_expert, keep)


def compact_kernel(place_ref, *refs):
    row_refs = refs[: 2 * GROUPS]
    packed_ref, spread_ref, scale_ref, pick_ref, weight_ref = refs[2 * GROUPS :]
    place_here = place_of(place_ref)
    half = BLOCKS // 2
    earlier = (
        lax.broadcasted_iota(jnp.int32, (ROWS, ROWS), 0)
        < lax.broadcasted_iota(jnp.int32, (ROWS, ROWS), 1)
    ).astype(BF16)
    rank = lax.broadcasted_iota(jnp.int32, (CAP, ROWS), 0).astype(F32)
    mine = lax.broadcasted_iota(jnp.int32, (BLOCKS, GROUP), 0) == 4 * place_here[0] + place_here[1]

    def fetch(ref, group, start, i):
        b = block_at(PLANS[group], place_here, start + i)
        parts = jnp.where(mine, ref[i, ROWS:].astype(F32), 0.0)
        parts = jnp.sum(parts, axis=0, keepdims=True)
        parts = [parts[:, n * ROWS : (n + 1) * ROWS] for n in range(6)]
        for n in range(2):
            s = 2 * group + n
            weight_ref[b, s : s + 1] = parts[3 * n] + parts[3 * n + 1] + parts[3 * n + 2]

    def choose(b):
        weight = weight_ref[b]
        hit = weight > 0.0
        place = jnp.dot(hit.astype(BF16), earlier, preferred_element_type=F32)
        place = jnp.where(hit, place, -1.0)
        picks = [rank == place[s : s + 1] for s in range(LOCAL)]
        for s in range(LOCAL):
            scale_ref[s, b] = jnp.sum(
                jnp.where(picks[s], weight[s : s + 1], 0.0), axis=1, keepdims=True
            )
        pick = jnp.concatenate([p.astype(F32) for p in picks], axis=0)
        spread_ref[b] = jnp.transpose(pick).astype(BF16)
        pick_ref[b] = pick.astype(BF16)

    def pack(ref, group, start, i):
        b = block_at(PLANS[group], place_here, start + i)
        packed = jnp.dot(pick_ref[b], ref[i, :ROWS], preferred_element_type=F32).astype(BF16)
        packed_ref[:, b, :, group * GROUP : (group + 1) * GROUP] = packed.reshape(
            LOCAL, CAP, GROUP
        )

    for n, ref in enumerate(row_refs):
        each(half, 2, functools.partial(fetch, ref, n // 2, n % 2 * half))
    each(BLOCKS, 2, choose)
    for n, ref in enumerate(row_refs):
        each(half, 2, functools.partial(pack, ref, n // 2, n % 2 * half))


def compact(place, rows):
    vmem = pl.BlockSpec(memory_space=pltpu.VMEM)
    return pl.pallas_call(
        compact_kernel,
        in_specs=[pl.BlockSpec(memory_space=pltpu.SMEM)] + [vmem] * len(rows),
        out_specs=[vmem] * 3,
        out_shape=[
            jax.ShapeDtypeStruct((LOCAL, BLOCKS, CAP, D), BF16),
            jax.ShapeDtypeStruct((BLOCKS, ROWS, LOCAL * CAP), BF16),
            jax.ShapeDtypeStruct((LOCAL, BLOCKS, CAP, 1), F32),
        ],
        scratch_shapes=[
            pltpu.VMEM((BLOCKS, LOCAL * CAP, ROWS), BF16),
            pltpu.VMEM((BLOCKS, LOCAL, ROWS), F32),
        ],
        compiler_params=params(24),
        name="compact",
    )(place, *rows)


def back_to_rows(plan, place, start, group, act_ref, down_ref, spread_ref, part_ref, out_refs):
    half = BLOCKS // 2
    order = [block_at(plan, place, start + i) for i in range(half)]
    for s in range(LOCAL):
        rows = jnp.concatenate([act_ref[s, b] for b in order])
        down = down_ref[group, s // 2, :, s % 2].reshape(GROUP, FF)
        part = lax.dot_general(
            rows, down, (((1,), (1,)), ((), ())), preferred_element_type=F32
        )
        part_ref[:, s] = part.astype(BF16).reshape(half, CAP, GROUP)

    def back(out_ref, first, i):
        b = block_at(plan, place, start + first + i)
        rows = part_ref[first + i].reshape(LOCAL * CAP, GROUP)
        out_ref[i] = jnp.dot(spread_ref[b], rows, preferred_element_type=F32).astype(BF16)

    for n, out_ref in enumerate(out_refs):
        each(half // 2, 4, functools.partial(back, out_ref, n * half // 2))


def experts_kernel(place_ref, packed_hbm, scale_hbm, spread_hbm, weights_hbm, *refs):
    out_refs, act_ref = refs[: 2 * GROUPS], refs[2 * GROUPS]
    packed_ref, scale_ref, gate_ref, up_ref, down_ref, spread_ref, part_ref = refs[2 * GROUPS + 1 : -3]
    slot_sems, down_sems, once_sems = refs[-3:]
    blks = 8 // GROUPS
    fetch = pltpu.make_async_copy
    by_slot = [
        [
            fetch(packed_hbm.at[s], packed_ref.at[s], slot_sems.at[s, 0]),
            fetch(weights_hbm.at[s // 2, :, 0, s % 2], gate_ref.at[s], slot_sems.at[s, 1]),
            fetch(weights_hbm.at[s // 2, :, 1, s % 2], up_ref.at[s], slot_sems.at[s, 2]),
        ]
        for s in range(LOCAL)
    ]
    by_group = [
        fetch(weights_hbm.at[:, blks * g : blks * (g + 1), 2], down_ref.at[g], down_sems.at[g])
        for g in range(GROUPS)
    ]
    scales = fetch(scale_hbm, scale_ref, once_sems.at[0])
    spreads = fetch(spread_hbm, spread_ref, once_sems.at[1])
    for copy in (*by_slot[0], scales, *by_slot[1], *by_slot[2], *by_slot[3], *by_group, spreads):
        copy.start()
    for s in range(LOCAL):
        by_slot[s][0].wait()
        by_slot[s][1].wait()
        rows = packed_ref[s].reshape(BLOCKS * CAP, D)
        gate = jnp.dot(rows, gate_ref[s].reshape(D, FF), preferred_element_type=F32)
        by_slot[s][2].wait()
        up = jnp.dot(rows, up_ref[s].reshape(D, FF), preferred_element_type=F32)
        if s == 0:
            scales.wait()
        scale = scale_ref[s].reshape(BLOCKS * CAP, 1)
        act = (gate / (1.0 + jnp.exp(-gate)) * up * scale).astype(BF16)
        act_ref[s] = act.reshape(BLOCKS, CAP, FF)
    spreads.wait()
    for g, plan in enumerate(PLANS):
        by_group[g].wait()
        back_to_rows(
            plan, place_of(place_ref), BLOCKS // 2, g, act_ref, down_ref, spread_ref, part_ref,
            out_refs[2 * g : 2 * g + 2],
        )


def experts(place, packed, scale, spread, weights):
    half = BLOCKS // 2
    vmem, hbm = pl.BlockSpec(memory_space=pltpu.VMEM), pl.BlockSpec(memory_space=pltpu.HBM)
    return pl.pallas_call(
        experts_kernel,
        in_specs=[pl.BlockSpec(memory_space=pltpu.SMEM), hbm, hbm, hbm, hbm],
        out_specs=[vmem] * (2 * GROUPS + 1),
        out_shape=[jax.ShapeDtypeStruct((half // 2, ROWS, GROUP), BF16)] * (2 * GROUPS)
        + [jax.ShapeDtypeStruct((LOCAL, BLOCKS, CAP, FF), BF16)],
        scratch_shapes=[
            pltpu.VMEM(packed.shape, BF16),
            pltpu.VMEM(scale.shape, F32),
            pltpu.VMEM((LOCAL, 8, CHUNK, FF), BF16),
            pltpu.VMEM((LOCAL, 8, CHUNK, FF), BF16),
            pltpu.VMEM((GROUPS, 2, 8 // GROUPS, 2, CHUNK, FF), BF16),
            pltpu.VMEM(spread.shape, BF16),
            pltpu.VMEM((half, LOCAL, CAP, GROUP), BF16),
            pltpu.SemaphoreType.DMA((LOCAL, 3)),
            pltpu.SemaphoreType.DMA((GROUPS,)),
            pltpu.SemaphoreType.DMA((2,)),
        ],
        compiler_params=params(48),
        name="experts",
    )(place, packed, scale, spread, weights)


def kept_kernel(place_ref, act_ref, spread_hbm, weights_hbm, *refs):
    out_refs, (down_ref, spread_ref, part_ref, sems) = refs[: 2 * GROUPS], refs[2 * GROUPS :]
    blks = 8 // GROUPS
    copies = [
        pltpu.make_async_copy(
            weights_hbm.at[:, blks * g : blks * (g + 1), 2], down_ref.at[g], sems.at[g]
        )
        for g in range(GROUPS)
    ]
    spreads = pltpu.make_async_copy(spread_hbm, spread_ref, sems.at[GROUPS])
    for copy in (copies[0], spreads, *copies[1:]):
        copy.start()
    spreads.wait()
    for g, plan in enumerate(PLANS):
        copies[g].wait()
        back_to_rows(
            plan, place_of(place_ref), 0, g, act_ref, down_ref, spread_ref, part_ref,
            out_refs[2 * g : 2 * g + 2],
        )


def kept(place, act, spread, weights):
    half = BLOCKS // 2
    vmem, hbm = pl.BlockSpec(memory_space=pltpu.VMEM), pl.BlockSpec(memory_space=pltpu.HBM)
    return pl.pallas_call(
        kept_kernel,
        in_specs=[pl.BlockSpec(memory_space=pltpu.SMEM), vmem, hbm, hbm],
        out_specs=[vmem] * (2 * GROUPS),
        out_shape=[jax.ShapeDtypeStruct((half // 2, ROWS, GROUP), BF16)] * (2 * GROUPS),
        scratch_shapes=[
            pltpu.VMEM((GROUPS, 2, 8 // GROUPS, 2, CHUNK, FF), BF16),
            pltpu.VMEM(spread.shape, BF16),
            pltpu.VMEM((half, LOCAL, CAP, GROUP), BF16),
            pltpu.SemaphoreType.DMA((GROUPS + 1,)),
        ],
        compiler_params=params(24),
        name="kept",
    )(place, act, spread, weights)


def closing_kernel(hidden_ref, gain_ref, *refs):
    parts, out_ref = refs[:-1], refs[-1]
    moe = sum(ref[...].astype(F32) for ref in parts)
    mixed = hidden_ref[...] + moe
    mean_sq = jnp.mean(mixed * mixed, axis=-1, keepdims=True)
    out_ref[...] = (mixed * lax.rsqrt(mean_sq + EPS) * gain_ref[...]).astype(BF16)


def closing(hidden, gain, parts):
    return pl.pallas_call(
        closing_kernel,
        out_shape=jax.ShapeDtypeStruct((ROWS, D), BF16),
        compiler_params=params(8),
        name="closing",
    )(hidden, gain, *parts)


def spread_out(rows):
    halves = []
    for group, (first, other) in enumerate(PLANS):
        held = rows[group][None]
        for turn, large in ((other, False), (first, False), (other, True)):
            held = jnp.concatenate([held, turned(held, turn, large)])
        halves += [held, turned(held, first, True)]
    return halves


def add(a, b):
    return (a.astype(F32) + b.astype(F32)).astype(BF16)


def body(
    attn_out, resid, w_o, norm1_gain, router_w, route_slot, slot_expert, keep,
    w_gate, w_up, w_down, norm2_gain,
):
    joined = join(w_gate, w_up, w_down)
    weights = lax.all_gather(joined, ("core", "blk"), axis=0, tiled=False)
    weights = weights.reshape(2, 8, 3, 2, CHUNK, FF)
    weights = pltpu.with_memory_space_constraint(weights, pltpu.HBM)

    hidden, outgoing = entry(
        attn_out, resid, w_o, norm1_gain.reshape(1, D), router_w.T, route_slot.T,
        slot_expert.reshape(1, SLOTS), keep.reshape(1, ROWS),
    )
    place = jnp.stack([lax.axis_index(name) for name in ("x", "y", "core")])
    place = place.astype(jnp.int32)
    packed, spread, scale = [
        pltpu.with_memory_space_constraint(array, pltpu.HBM)
        for array in compact(place, spread_out(outgoing))
    ]
    *sends, act = experts(place, packed, scale, spread, weights)
    keeps = kept(place, act, spread, weights)
    sums = []
    for group, (first, other) in enumerate(PLANS):
        last, soon = sends[2 * group : 2 * group + 2]
        held, passed = keeps[2 * group : 2 * group + 2]
        passed = add(passed, turned(soon, first, True))
        held = add(held, turned(last, first, True))
        got = turned(passed, other, True)
        at = {0: 0, other: 1, first: 2, first ^ other: 3}
        sums.append([add(held[at[turn]], got[at[turn]]) for turn in range(4)])
    parts = [jnp.concatenate(both, axis=1) for both in zip(*sums)]
    parts = parts[:1] + [turned(parts[turn], turn, False) for turn in (2, 1, 3)]
    return closing(hidden, norm2_gain.reshape(1, D), parts)


def solution(mesh):
    fine = Mesh(mesh.devices.reshape(4, 4, 2, 8), ("x", "y", "core", "blk"))
    rows = P(("x", "y", "core", "blk"), None)
    slots = P(("x", "y", "core"), "blk", None)
    placed = (
        rows, rows, P(), P(), P(), rows, P(), P(("x", "y", "core", "blk")),
        slots, slots, slots, P(),
    )
    return jax.shard_map(body, mesh=fine, in_specs=placed, out_specs=rows, check_vma=False)
```

```python
import functools

import jax
import jax.numpy as jnp
from jax import lax
from jax.experimental import pallas as pl
from jax.experimental.pallas import tpu as pltpu
from jax.sharding import Mesh
from jax.sharding import PartitionSpec as P

EPS = 1e-05
D = 1536
FF = 512
TOP = 8
SLOTS = 64
ROWS = 128
CAP = 32
BLOCKS = 16
LOCAL = 4
CHUNK = D // 8
GROUPS = 2
GROUP = D // GROUPS
F32 = jnp.float32
BF16 = jnp.bfloat16
MIB = 1024 * 1024


def params(mib, *semantics):
    return pltpu.CompilerParams(
        dimension_semantics=semantics or None, vmem_limit_bytes=mib * MIB
    )


PLANS = ((1, 3), (3, 1))


def block_at(plan, place, j):
    first, other = plan
    x, y, core = place
    bit = lambda n: (j >> n) & 1
    low = bit(0) * other ^ bit(1) * first
    high = bit(2) * other ^ bit(3) * first
    along_x = jnp.where(core == 0, high, low)
    along_y = jnp.where(core == 0, low, high)
    return 4 * (x ^ along_x) + (y ^ along_y)


def place_of(place_ref):
    return place_ref[0], place_ref[1], place_ref[2]


def turned(rows, turn, large):
    pairs = []
    for x in range(4):
        for y in range(4):
            for core in range(2):
                along_x = large == (core == 0)
                to = (x ^ turn, y) if along_x else (x, y ^ turn)
                pairs.append((8 * x + 2 * y + core, 8 * to[0] + 2 * to[1] + core))
    return lax.ppermute(rows, ("x", "y", "core"), pairs)


def each(count, unroll, step):
    def run(i, carry):
        step(i)
        return carry

    lax.fori_loop(0, count, run, 0, unroll=unroll)


def join_kernel(*refs):
    count = len(refs) - 3
    shards, joined, held, sems = refs[:count], refs[count], refs[count + 1], refs[count + 2]
    inward = [
        pltpu.make_async_copy(shard, held.at[n], sems.at[0, n]) for n, shard in enumerate(shards)
    ]
    outward = [
        pltpu.make_async_copy(held.at[n], joined.at[n], sems.at[1, n]) for n in range(count)
    ]
    for copy in inward:
        copy.start()
    for n in range(count):
        inward[n].wait()
        outward[n].start()
    for copy in outward:
        copy.wait()


def join(*shards):
    hbm = pl.BlockSpec(memory_space=pltpu.HBM)
    shape = (len(shards), *shards[0].shape)
    return pl.pallas_call(
        join_kernel,
        in_specs=[hbm] * len(shards),
        out_specs=hbm,
        out_shape=jax.ShapeDtypeStruct(shape, BF16),
        scratch_shapes=[pltpu.VMEM(shape, BF16), pltpu.SemaphoreType.DMA((2, len(shards)))],
        name="join",
    )(*shards)


def entry_kernel(
    attn_ref, resid_ref, wo_ref, gain_ref, router_ref, route_ref, expert_ref, keep_ref,
    hidden_ref, rows_ref,
):
    step = pl.program_id(0)
    width = wo_ref.shape[1]
    cols = pl.ds(step * width, width)
    hidden_ref[:, cols] = resid_ref[...].astype(F32) + jnp.dot(
        attn_ref[...], wo_ref[...], preferred_element_type=F32
    )

    @pl.when(step == pl.num_programs(0) - 1)
    def _():
        values = hidden_ref[...]
        mean_sq = jnp.mean(values * values, axis=-1, keepdims=True)
        normed = (values * lax.rsqrt(mean_sq + EPS) * gain_ref[...]).astype(BF16)
        logits = lax.dot_general(
            router_ref[...], normed.astype(F32), (((1,), (1,)), ((), ())),
            precision=lax.Precision.HIGHEST, preferred_element_type=F32,
        )
        experts = logits.shape[0]
        pick = lax.broadcasted_iota(jnp.int32, (experts, SLOTS), 0) == expert_ref[...]
        by_slot = lax.dot_general(
            pick.astype(F32), logits, (((0,), (0,)), ((), ())),
            precision=lax.Precision.HIGHEST, preferred_element_type=F32,
        )
        slot = lax.broadcasted_iota(jnp.int32, (SLOTS, ROWS), 0)
        named = slot == route_ref[0:1]
        for k in range(1, TOP):
            named = named | (slot == route_ref[k : k + 1])
        top = jnp.max(jnp.where(named, by_slot, -jnp.inf), axis=0, keepdims=True)
        grown = jnp.where(named, jnp.exp(jnp.where(named, by_slot - top, 0.0)), 0.0)
        probs = grown / jnp.sum(grown, axis=0, keepdims=True)
        live = jnp.where(keep_ref[...] > 0, probs, 0.0).reshape(BLOCKS, LOCAL, ROWS)
        for group in range(GROUPS):
            rows_ref[group, :ROWS] = normed[:, group * GROUP : (group + 1) * GROUP]
        for s in range(LOCAL):
            rest = live[:, s]
            for n in range(3):
                part = rest.astype(BF16)
                at = (s % 2 * 3 + n) * ROWS
                rows_ref[s // 2, ROWS:, at : at + ROWS] = part
                rest = rest - part.astype(F32)


def entry(attn_out, resid, w_o, gain, router_w, route_slot, slot_expert, keep):
    steps = 6
    width = D // steps
    whole = lambda shape: pl.BlockSpec(shape, lambda i: (0,) * len(shape))
    return pl.pallas_call(
        entry_kernel,
        grid=(steps,),
        in_specs=[
            whole((ROWS, D)),
            pl.BlockSpec((ROWS, width), lambda i: (0, i)),
            pl.BlockSpec((D, width), lambda i: (0, i)),
            whole(gain.shape),
            whole(router_w.shape),
            whole(route_slot.shape),
            whole(slot_expert.shape),
            whole(keep.shape),
        ],
        out_specs=[whole((ROWS, D)), whole((GROUPS, ROWS + BLOCKS, GROUP))],
        out_shape=[
            jax.ShapeDtypeStruct((ROWS, D), F32),
            jax.ShapeDtypeStruct((GROUPS, ROWS + BLOCKS, GROUP), BF16),
        ],
        compiler_params=params(16, "arbitrary"),
        name="entry",
    )(attn_out, resid, w_o, gain, router_w, route_slot, slot_expert, keep)


def compact_kernel(place_ref, *refs):
    row_refs = refs[: 2 * GROUPS]
    packed_ref, spread_ref, scale_ref, pick_ref, weight_ref = refs[2 * GROUPS :]
    place_here = place_of(place_ref)
    half = BLOCKS // 2
    earlier = (
        lax.broadcasted_iota(jnp.int32, (ROWS, ROWS), 0)
        < lax.broadcasted_iota(jnp.int32, (ROWS, ROWS), 1)
    ).astype(BF16)
    rank = lax.broadcasted_iota(jnp.int32, (CAP, ROWS), 0).astype(F32)
    mine = lax.broadcasted_iota(jnp.int32, (BLOCKS, GROUP), 0) == 4 * place_here[0] + place_here[1]

    def fetch(ref, group, start, i):
        b = block_at(PLANS[group], place_here, start + i)
        parts = jnp.where(mine, ref[i, ROWS:].astype(F32), 0.0)
        parts = jnp.sum(parts, axis=0, keepdims=True)
        parts = [parts[:, n * ROWS : (n + 1) * ROWS] for n in range(6)]
        for n in range(2):
            s = 2 * group + n
            weight_ref[b, s : s + 1] = parts[3 * n] + parts[3 * n + 1] + parts[3 * n + 2]

    def choose(b):
        weight = weight_ref[b]
        hit = weight > 0.0
        place = jnp.dot(hit.astype(BF16), earlier, preferred_element_type=F32)
        place = jnp.where(hit, place, -1.0)
        picks = [rank == place[s : s + 1] for s in range(LOCAL)]
        for s in range(LOCAL):
            scale_ref[s, b] = jnp.sum(
                jnp.where(picks[s], weight[s : s + 1], 0.0), axis=1, keepdims=True
            )
        pick = jnp.concatenate([p.astype(F32) for p in picks], axis=0)
        spread_ref[b] = jnp.transpose(pick).astype(BF16)
        pick_ref[b] = pick.astype(BF16)

    def pack(ref, group, start, i):
        b = block_at(PLANS[group], place_here, start + i)
        packed = jnp.dot(pick_ref[b], ref[i, :ROWS], preferred_element_type=F32).astype(BF16)
        packed_ref[:, b, :, group * GROUP : (group + 1) * GROUP] = packed.reshape(
            LOCAL, CAP, GROUP
        )

    for n, ref in enumerate(row_refs):
        each(half, 2, functools.partial(fetch, ref, n // 2, n % 2 * half))
    each(BLOCKS, 2, choose)
    for n, ref in enumerate(row_refs):
        each(half, 2, functools.partial(pack, ref, n // 2, n % 2 * half))


def compact(place, rows):
    vmem = pl.BlockSpec(memory_space=pltpu.VMEM)
    return pl.pallas_call(
        compact_kernel,
        in_specs=[pl.BlockSpec(memory_space=pltpu.SMEM)] + [vmem] * len(rows),
        out_specs=[vmem] * 3,
        out_shape=[
            jax.ShapeDtypeStruct((LOCAL, BLOCKS, CAP, D), BF16),
            jax.ShapeDtypeStruct((BLOCKS, ROWS, LOCAL * CAP), BF16),
            jax.ShapeDtypeStruct((LOCAL, BLOCKS, CAP, 1), F32),
        ],
        scratch_shapes=[
            pltpu.VMEM((BLOCKS, LOCAL * CAP, ROWS), BF16),
            pltpu.VMEM((BLOCKS, LOCAL, ROWS), F32),
        ],
        compiler_params=params(24),
        name="compact",
    )(place, *rows)


def back_to_rows(plan, place, start, group, act_ref, down_ref, spread_ref, part_ref, out_refs):
    half = BLOCKS // 2
    order = [block_at(plan, place, start + i) for i in range(half)]
    for s in range(LOCAL):
        rows = jnp.concatenate([act_ref[s, b] for b in order])
        down = down_ref[group, s // 2, :, s % 2].reshape(GROUP, FF)
        part = lax.dot_general(
            rows, down, (((1,), (1,)), ((), ())), preferred_element_type=F32
        )
        part_ref[:, s] = part.astype(BF16).reshape(half, CAP, GROUP)

    def back(out_ref, first, i):
        b = block_at(plan, place, start + first + i)
        rows = part_ref[first + i].reshape(LOCAL * CAP, GROUP)
        out_ref[i] = jnp.dot(spread_ref[b], rows, preferred_element_type=F32).astype(BF16)

    for n, out_ref in enumerate(out_refs):
        each(half // 2, 4, functools.partial(back, out_ref, n * half // 2))


def experts_kernel(place_ref, packed_hbm, scale_hbm, spread_hbm, weights_hbm, *refs):
    out_refs, act_ref = refs[: 2 * GROUPS], refs[2 * GROUPS]
    packed_ref, scale_ref, gate_ref, up_ref, down_ref, spread_ref, part_ref = refs[2 * GROUPS + 1 : -3]
    slot_sems, down_sems, once_sems = refs[-3:]
    blks = 8 // GROUPS
    fetch = pltpu.make_async_copy
    by_slot = [
        [
            fetch(packed_hbm.at[s], packed_ref.at[s], slot_sems.at[s, 0]),
            fetch(weights_hbm.at[s // 2, :, 0, s % 2], gate_ref.at[s], slot_sems.at[s, 1]),
            fetch(weights_hbm.at[s // 2, :, 1, s % 2], up_ref.at[s], slot_sems.at[s, 2]),
        ]
        for s in range(LOCAL)
    ]
    by_group = [
        fetch(weights_hbm.at[:, blks * g : blks * (g + 1), 2], down_ref.at[g], down_sems.at[g])
        for g in range(GROUPS)
    ]
    scales = fetch(scale_hbm, scale_ref, once_sems.at[0])
    spreads = fetch(spread_hbm, spread_ref, once_sems.at[1])
    queue = [by_slot[0], [scales, *by_slot[1]], by_slot[2], by_slot[3], [*by_group, spreads]]
    for copy in (*queue[0], *queue[1]):
        copy.start()
    for s in range(LOCAL):
        by_slot[s][0].wait()
        by_slot[s][1].wait()
        for copy in queue[s + 2] if s + 2 < len(queue) else ():
            copy.start()
        rows = packed_ref[s].reshape(BLOCKS * CAP, D)
        gate = jnp.dot(rows, gate_ref[s].reshape(D, FF), preferred_element_type=F32)
        by_slot[s][2].wait()
        up = jnp.dot(rows, up_ref[s].reshape(D, FF), preferred_element_type=F32)
        if s == 0:
            scales.wait()
        scale = scale_ref[s].reshape(BLOCKS * CAP, 1)
        act = (gate / (1.0 + jnp.exp(-gate)) * up * scale).astype(BF16)
        act_ref[s] = act.reshape(BLOCKS, CAP, FF)
    spreads.wait()
    for g, plan in enumerate(PLANS):
        by_group[g].wait()
        back_to_rows(
            plan, place_of(place_ref), BLOCKS // 2, g, act_ref, down_ref, spread_ref, part_ref,
            out_refs[2 * g : 2 * g + 2],
        )


def experts(place, packed, scale, spread, weights):
    half = BLOCKS // 2
    vmem, hbm = pl.BlockSpec(memory_space=pltpu.VMEM), pl.BlockSpec(memory_space=pltpu.HBM)
    return pl.pallas_call(
        experts_kernel,
        in_specs=[pl.BlockSpec(memory_space=pltpu.SMEM), hbm, hbm, hbm, hbm],
        out_specs=[vmem] * (2 * GROUPS + 1),
        out_shape=[jax.ShapeDtypeStruct((half // 2, ROWS, GROUP), BF16)] * (2 * GROUPS)
        + [jax.ShapeDtypeStruct((LOCAL, BLOCKS, CAP, FF), BF16)],
        scratch_shapes=[
            pltpu.VMEM(packed.shape, BF16),
            pltpu.VMEM(scale.shape, F32),
            pltpu.VMEM((LOCAL, 8, CHUNK, FF), BF16),
            pltpu.VMEM((LOCAL, 8, CHUNK, FF), BF16),
            pltpu.VMEM((GROUPS, 2, 8 // GROUPS, 2, CHUNK, FF), BF16),
            pltpu.VMEM(spread.shape, BF16),
            pltpu.VMEM((half, LOCAL, CAP, GROUP), BF16),
            pltpu.SemaphoreType.DMA((LOCAL, 3)),
            pltpu.SemaphoreType.DMA((GROUPS,)),
            pltpu.SemaphoreType.DMA((2,)),
        ],
        compiler_params=params(48),
        name="experts",
    )(place, packed, scale, spread, weights)


def kept_kernel(place_ref, act_ref, spread_hbm, weights_hbm, *refs):
    out_refs, (down_ref, spread_ref, part_ref, sems) = refs[: 2 * GROUPS], refs[2 * GROUPS :]
    blks = 8 // GROUPS
    copies = [
        pltpu.make_async_copy(
            weights_hbm.at[:, blks * g : blks * (g + 1), 2], down_ref.at[g], sems.at[g]
        )
        for g in range(GROUPS)
    ]
    spreads = pltpu.make_async_copy(spread_hbm, spread_ref, sems.at[GROUPS])
    for copy in (copies[0], spreads, *copies[1:]):
        copy.start()
    spreads.wait()
    for g, plan in enumerate(PLANS):
        copies[g].wait()
        back_to_rows(
            plan, place_of(place_ref), 0, g, act_ref, down_ref, spread_ref, part_ref,
            out_refs[2 * g : 2 * g + 2],
        )


def kept(place, act, spread, weights):
    half = BLOCKS // 2
    vmem, hbm = pl.BlockSpec(memory_space=pltpu.VMEM), pl.BlockSpec(memory_space=pltpu.HBM)
    return pl.pallas_call(
        kept_kernel,
        in_specs=[pl.BlockSpec(memory_space=pltpu.SMEM), vmem, hbm, hbm],
        out_specs=[vmem] * (2 * GROUPS),
        out_shape=[jax.ShapeDtypeStruct((half // 2, ROWS, GROUP), BF16)] * (2 * GROUPS),
        scratch_shapes=[
            pltpu.VMEM((GROUPS, 2, 8 // GROUPS, 2, CHUNK, FF), BF16),
            pltpu.VMEM(spread.shape, BF16),
            pltpu.VMEM((half, LOCAL, CAP, GROUP), BF16),
            pltpu.SemaphoreType.DMA((GROUPS + 1,)),
        ],
        compiler_params=params(24),
        name="kept",
    )(place, act, spread, weights)


def closing_kernel(hidden_ref, gain_ref, *refs):
    parts, out_ref = refs[:-1], refs[-1]
    moe = sum(ref[...].astype(F32) for ref in parts)
    mixed = hidden_ref[...] + moe
    mean_sq = jnp.mean(mixed * mixed, axis=-1, keepdims=True)
    out_ref[...] = (mixed * lax.rsqrt(mean_sq + EPS) * gain_ref[...]).astype(BF16)


def closing(hidden, gain, parts):
    return pl.pallas_call(
        closing_kernel,
        out_shape=jax.ShapeDtypeStruct((ROWS, D), BF16),
        compiler_params=params(8),
        name="closing",
    )(hidden, gain, *parts)


def spread_out(rows):
    halves = []
    for group, (first, other) in enumerate(PLANS):
        held = rows[group][None]
        for turn, large in ((other, False), (first, False), (other, True)):
            held = jnp.concatenate([held, turned(held, turn, large)])
        halves += [held, turned(held, first, True)]
    return halves


def add(a, b):
    return (a.astype(F32) + b.astype(F32)).astype(BF16)


def body(
    attn_out, resid, w_o, norm1_gain, router_w, route_slot, slot_expert, keep,
    w_gate, w_up, w_down, norm2_gain,
):
    joined = join(w_gate, w_up, w_down)
    weights = lax.all_gather(joined, ("core", "blk"), axis=0, tiled=False)
    weights = weights.reshape(2, 8, 3, 2, CHUNK, FF)
    weights = pltpu.with_memory_space_constraint(weights, pltpu.HBM)

    hidden, outgoing = entry(
        attn_out, resid, w_o, norm1_gain.reshape(1, D), router_w.T, route_slot.T,
        slot_expert.reshape(1, SLOTS), keep.reshape(1, ROWS),
    )
    place = jnp.stack([lax.axis_index(name) for name in ("x", "y", "core")])
    place = place.astype(jnp.int32)
    packed, spread, scale = [
        pltpu.with_memory_space_constraint(array, pltpu.HBM)
        for array in compact(place, spread_out(outgoing))
    ]
    *sends, act = experts(place, packed, scale, spread, weights)
    keeps = kept(place, act, spread, weights)
    sums = []
    for group, (first, other) in enumerate(PLANS):
        last, soon = sends[2 * group : 2 * group + 2]
        held, passed = keeps[2 * group : 2 * group + 2]
        passed = add(passed, turned(soon, first, True))
        held = add(held, turned(last, first, True))
        got = turned(passed, other, True)
        at = {0: 0, other: 1, first: 2, first ^ other: 3}
        sums.append([add(held[at[turn]], got[at[turn]]) for turn in range(4)])
    parts = [jnp.concatenate(both, axis=1) for both in zip(*sums)]
    parts = parts[:1] + [turned(parts[turn], turn, False) for turn in (2, 1, 3)]
    return closing(hidden, norm2_gain.reshape(1, D), parts)


def solution(mesh):
    fine = Mesh(mesh.devices.reshape(4, 4, 2, 8), ("x", "y", "core", "blk"))
    rows = P(("x", "y", "core", "blk"), None)
    slots = P(("x", "y", "core"), "blk", None)
    placed = (
        rows, rows, P(), P(), P(), rows, P(), P(("x", "y", "core", "blk")),
        slots, slots, slots, P(),
    )
    return jax.shard_map(body, mesh=fine, in_specs=placed, out_specs=rows, check_vma=False)
```
